32 devices in a mesh: req: 8 (over z, x), head: 4 (over y, core).
Axes of the slice: x: 2, y: 2, z: 4, core: 2. Of those that a mesh axis runs over, the one named last changes fastest.
Arguments:
- hidden_in: bfloat16 [8, 512, 2048], P('req', 'head'), may hold values from -16 to 16
- norm_gain: float32 [2048], replicated, may hold values from 0.1 to 1.9
- query_weight: bfloat16 [2048, 2048], P(None, 'head'), may hold values from -0.25 to 0.25
- key_weight: bfloat16 [2048, 512], P(None, 'head'), may hold values from -0.125 to 0.125
- value_weight: bfloat16 [2048, 512], P(None, 'head'), may hold values from -0.125 to 0.125
- output_weight: bfloat16 [2048, 2048], P('head'), may hold values from -0.75 to 0.75
- cache_keys: bfloat16 [8, 4096, 512], P('req', None, 'head'), may hold values from -256 to 256
- cache_values: bfloat16 [8, 4096, 512], P('req', None, 'head'), may hold values from -6 to 6
- held_states: bfloat16 [8, 384, 2048], P('req'), may hold values from -6 to 6
- cache_lengths: int32 [8], P('req'), may hold values from 512 to 4096, as said below
- recompute_index: int32 [8, 384], P('req'), may hold values from 0 to 4095, as said below
- slot_request: int32 [8], replicated, may hold values from 0 to 7, each once
Outputs:
- hidden_out: bfloat16 [8, 512, 2048], P('req', 'head')
- new_keys: bfloat16 [8, 512, 512], P('req', None, 'head')
- new_values: bfloat16 [8, 512, 512], P('req', None, 'head')
The draws below stay inside these ranges and needn't reach their ends.
Inputs may be any that keep to these rules, and one draw needn't show every extreme that they name: `cache_lengths`: each slot's length; one slot holds exactly 4096 and one exactly 512. `recompute_index`: each slot's 384 entries are distinct positions below that slot's cache length. A permutation: slot s serves request slot_request[s].
All inputs are finite; a program needn't handle non-finite values.
Results may differ from the reference program's by a relative error of at most 0.018.
The reference program's roundings to bfloat16 on the way count: a program that leaves them out, or rounds other values in their place, can miss the bound.
Values may be sent and summed in bfloat16 or wider, within the bound.
No kernel may reach another device: no remote copies, remote signals or barrier semaphores. Data moves between devices by JAX's collectives and lax.ppermute only.
A program may use at most 64 MiB of HBM per device.

```python
import math
import jax
import jax.numpy as jnp
from jax import lax

D = 2048
H = 32
KVH = 8
HD = 64
NEW = 512
CACHE = 4096
RECOMP = 384
REQS = 8
N_HEAD = 4


def draw_hidden_in(key, part):
    column_key = jax.random.fold_in(key, 0)
    entry_key = jax.random.fold_in(key, 3)
    columns = jnp.exp(jax.random.uniform(column_key, (D,), jnp.float32, math.log(0.25), math.log(2.5)))
    values = jnp.clip(jax.random.normal(entry_key, (REQS, NEW, D), jnp.float32), -4.0, 4.0) * columns
    return values.astype(jnp.bfloat16)


def draw_cache_keys(key, part):
    width_all = KVH * HD
    pairs = CACHE // 2
    drawn_key = jax.random.fold_in(jax.random.fold_in(key, 11), 1)
    values = jnp.clip(jax.random.normal(drawn_key, (REQS, pairs, 2, width_all), jnp.float32), -6.0, 6.0)
    return values.reshape(REQS, CACHE, width_all).astype(jnp.bfloat16)


def lengths_and_picks(key):
    base_key = jax.random.fold_in(key, 31)
    first_key, top_key, low_key, pick_key = jax.random.split(base_key, 4)
    shortest = CACHE // 8
    lengths = jax.random.randint(first_key, (REQS,), shortest, CACHE + 1)
    top_slot = jax.random.randint(top_key, (), 0, REQS)
    low_slot = (top_slot + 1 + jax.random.randint(low_key, (), 0, REQS - 1)) % REQS
    lengths = lengths.at[top_slot].set(CACHE).at[low_slot].set(shortest)
    row_keys = jax.random.split(pick_key, REQS)
    shuffled = jax.vmap(lambda row_key: jax.random.permutation(row_key, CACHE))(row_keys).astype(jnp.int32)
    outside = (shuffled >= lengths[:, None]).astype(jnp.int32)
    is_top = (jnp.arange(REQS) == top_slot)[:, None]
    forced = (is_top & ((shuffled == 0) | (shuffled == CACHE - 1))).astype(jnp.int32)
    ranking = outside * 2 + 1 - forced
    ordering = jnp.argsort(ranking, axis=1, stable=True)
    picks = jnp.take_along_axis(shuffled, ordering[:, :RECOMP], axis=1)
    return (lengths.astype(jnp.int32), picks.astype(jnp.int32))


def draw_cache_lengths(key, part):
    return lengths_and_picks(key)[0]


def draw_recompute_index(key, part):
    return lengths_and_picks(key)[1]


def steps_of(rng, extent, shards, least, high):
    def one(dim, shards_of):
        steps = jax.random.uniform(jax.random.fold_in(jax.random.fold_in(rng, 6), dim), (shards_of,), jnp.float32, least / len(shards), high / len(shards))
        return jnp.repeat(jnp.exp(steps), extent[dim] // shards_of).reshape((-1,) + (1,) * (len(extent) - dim - 1))

    loudness = one(*shards[0])
    for cut in shards[1:]:
        loudness = loudness * one(*cut)
    return loudness


def bell_draw(rng, shape, scale, reach, cuts=(), kind=jnp.bfloat16):
    drawn = scale * jax.random.normal(rng, shape, jnp.float32)
    if cuts:
        drawn = drawn * steps_of(rng, shape, cuts, -0.22, 0.18)
    return jnp.clip(drawn, -reach, reach).astype(kind)


def setup_inputs(seed: int = 0) -> dict:
    streams_of = jax.random.split(jax.random.key(seed), 13)
    return {
        "hidden_in": draw_hidden_in(jax.random.fold_in(streams_of[12], 71), 0),
        "norm_gain": jnp.clip(1.0 + 0.18 * jax.random.normal(streams_of[1], (D,), jnp.float32), 0.1, 1.9),
        "query_weight": bell_draw(streams_of[2], (D, H * HD), (D // 4) ** -0.5, 0.25, ((1, 4),)),
        "key_weight": bell_draw(streams_of[3], (D, KVH * HD), D ** -0.5, 0.125, ((1, 4),)),
        "value_weight": bell_draw(streams_of[4], (D, KVH * HD), D ** -0.5, 0.125, ((1, 4),)),
        "output_weight": bell_draw(streams_of[5], (H * HD, D), (H * HD // 32) ** -0.5, 0.75, ((0, 4),)),
        "cache_keys": draw_cache_keys(jax.random.fold_in(streams_of[12], 71), 0),
        "cache_values": bell_draw(streams_of[7], (REQS, CACHE, KVH * HD), 1.0, 6.0, ((0, 8), (2, 4))),
        "held_states": bell_draw(streams_of[8], (REQS, RECOMP, D), 1.0, 6.0, ((0, 8),)),
        "cache_lengths": draw_cache_lengths(jax.random.fold_in(streams_of[12], 71), 0),
        "recompute_index": draw_recompute_index(jax.random.fold_in(streams_of[12], 71), 0),
        "slot_request": jax.random.permutation(streams_of[11], REQS).astype(jnp.int32),
    }


rope_base = 500000.0

def rms_scaled(matrix, gains):
    values = matrix.astype(jnp.float32)
    factor = lax.rsqrt(lax.optimization_barrier(jnp.mean(values * values, axis=-1, keepdims=True)) + 1e-05)
    return (values * factor * gains).astype(jnp.bfloat16)

def rotate(vectors, positions):
    halfway = vectors.shape[-1] // 2
    ladder = jnp.arange(halfway).astype(jnp.float32)
    frequency = jnp.exp(ladder * (-2.0 * math.log(rope_base) / vectors.shape[-1]))
    angles = positions[..., None, None] * frequency
    cosine = jnp.cos(angles)
    sine_part = jnp.sin(angles)
    former = vectors[..., :halfway]
    latter = vectors[..., halfway:]
    return jnp.concatenate([former * cosine - latter * sine_part, latter * cosine + former * sine_part], axis=-1)

def reference(hidden_in, norm_gain, query_weight, key_weight, value_weight, output_weight, cache_keys, cache_values, held_states, cache_lengths, recompute_index, slot_request):
    per_group = H // KVH
    scaled = HD ** (-0.5)
    normed = rms_scaled(hidden_in, norm_gain)
    slotted = jnp.take(normed, slot_request, axis=0).reshape(REQS * NEW, D)
    query_raw = jnp.dot(slotted, query_weight, preferred_element_type=jnp.float32).reshape(REQS, NEW, H, HD)
    key_raw = jnp.dot(slotted, key_weight, preferred_element_type=jnp.float32).reshape(REQS, NEW, KVH, HD)
    value_raw = jnp.dot(slotted, value_weight, preferred_element_type=jnp.float32)
    spots = cache_lengths.astype(jnp.float32)[:, None] + jnp.arange(NEW).astype(jnp.float32)[None, :]
    queries = rotate(query_raw, spots).astype(jnp.bfloat16)
    new_keys = rotate(key_raw, spots).astype(jnp.bfloat16).reshape(REQS, NEW, KVH * HD)
    new_values = value_raw.astype(jnp.bfloat16).reshape(REQS, NEW, KVH * HD)
    held_normed = rms_scaled(held_states, norm_gain).reshape(REQS * RECOMP, D)
    held_key_raw = jnp.dot(held_normed, key_weight, preferred_element_type=jnp.float32).reshape(REQS, RECOMP, KVH, HD)
    held_keys = rotate(held_key_raw, recompute_index.astype(jnp.float32)).astype(jnp.bfloat16).reshape(REQS, RECOMP, KVH * HD)
    held_values = jnp.dot(held_normed, value_weight, preferred_element_type=jnp.float32).astype(jnp.bfloat16).reshape(REQS, RECOMP, KVH * HD)
    place = jax.vmap(lambda initial, indices, fresh_rows: initial.at[indices].set(fresh_rows))
    keys_all = jnp.concatenate([place(cache_keys, recompute_index, held_keys), new_keys], axis=1)
    values_all = jnp.concatenate([place(cache_values, recompute_index, held_values), new_values], axis=1)
    causal = jnp.arange(NEW)[None, :] <= jnp.arange(NEW)[:, None]

    def attend(item):
        query_rows, key_rows, value_rows, length_now = item
        allowed = jnp.concatenate([jnp.broadcast_to(jnp.arange(CACHE)[None, :] < length_now, (NEW, CACHE)), causal], axis=1)
        query_rows = query_rows.reshape(NEW, KVH, per_group, HD).astype(jnp.float32)
        key_rows = key_rows.reshape(CACHE + NEW, KVH, HD).astype(jnp.float32)
        value_rows = value_rows.reshape(CACHE + NEW, KVH, HD).astype(jnp.float32)

        def per_head(bundle):
            query_head, key_head, value_head = bundle
            scores = jnp.einsum('tgd,kd->gtk', query_head, key_head) * scaled
            scores = jnp.where(allowed[None], scores, -1e+30)
            highest = lax.optimization_barrier(jnp.max(scores, axis=-1, keepdims=True))
            weights = jnp.where(allowed[None], jnp.exp(scores - highest), 0.0)
            denominators = lax.optimization_barrier(jnp.sum(weights, axis=-1, keepdims=True))
            rounded_weights = lax.optimization_barrier(weights.astype(jnp.bfloat16)).astype(jnp.float32)
            summed_values = jnp.einsum('gtk,kd->tgd', rounded_weights, value_head)
            return summed_values / jnp.transpose(denominators, (1, 0, 2))
        heads_out = lax.map(per_head, (jnp.transpose(query_rows, (1, 0, 2, 3)), jnp.transpose(key_rows, (1, 0, 2)), jnp.transpose(value_rows, (1, 0, 2))))
        return jnp.transpose(heads_out, (1, 0, 2, 3)).reshape(NEW, H * HD).astype(jnp.bfloat16)
    attended = lax.map(attend, (queries, keys_all, values_all, cache_lengths))
    columns_each = H * HD // N_HEAD
    flat_rows = attended.reshape(REQS * NEW, H * HD)
    summed = jnp.zeros((REQS * NEW, D), jnp.float32)
    for group_index in range(N_HEAD):
        lower = group_index * columns_each
        upper = lower + columns_each
        group_term = jnp.dot(flat_rows[:, lower:upper], output_weight[lower:upper], preferred_element_type=jnp.float32)
        summed = summed + lax.optimization_barrier(group_term.astype(jnp.bfloat16)).astype(jnp.float32)
    projected = summed.astype(jnp.bfloat16).reshape(REQS, NEW, D)
    inverse = jnp.zeros((REQS,), jnp.int32).at[slot_request].set(jnp.arange(REQS).astype(jnp.int32))
    returned = jnp.take(projected, inverse, axis=0)
    hidden_out = (hidden_in.astype(jnp.float32) + returned.astype(jnp.float32)).astype(jnp.bfloat16)
    return (hidden_out, new_keys, new_values)
```

```python
import functools, math
import jax
import jax.numpy as jnp
from jax import lax
from jax.experimental import pallas as pl
from jax.experimental.pallas import tpu as pltpu
from jax.sharding import PartitionSpec as P

HD = 64
LANES = 128
F32 = jnp.float32
BF16 = jnp.bfloat16
ROPE_BASE = 500000.0
MASKED = -1e30
TOP = 2.0**100
FACTOR = HD**-0.5 * math.log2(math.e)
NT = (((1,), (1,)), ((), ()))
VM = pl.BlockSpec(memory_space=pltpu.VMEM)
SM = pl.BlockSpec(memory_space=pltpu.SMEM)


def rms_scaled(values, gains):
    factor = lax.rsqrt(jnp.mean(values * values, axis=-1, keepdims=True) + 1e-05)
    return (values * factor * gains).astype(BF16)


def lane_of(shape):
    return lax.broadcasted_iota(jnp.int32, shape, len(shape) - 1)


def turned(x, cosine, sine):
    lane = lane_of(x.shape)
    swapped = jnp.where(
        lane % HD < HD // 2, pltpu.roll(x, LANES - HD // 2, 1), pltpu.roll(x, HD // 2, 1)
    )
    return x * cosine + swapped * sine


def head_lanes(x, which):
    return x if which == 0 else pltpu.roll(x, HD, 1)


def key_rows(k, which, bias):
    lane = lane_of(k.shape)
    tail = jnp.where(lane == HD, 1.0, jnp.where(lane == HD + 1, bias, 0.0))
    return jnp.where(lane < HD, head_lanes(k, which), tail).astype(BF16)


def value_rows(v, which):
    lane = lane_of(v.shape)
    return jnp.where(lane < HD, head_lanes(v, which), jnp.where(lane == HD, 1.0, 0.0)).astype(BF16)


def prep_kernel(length, held, gain, wk, wv, cosine, sine, index, ck, cv, ka, va, fresh):
    normed = rms_scaled(held[...].astype(F32), gain[...])
    k = jnp.dot(normed, wk[...], preferred_element_type=F32)
    fresh[:, :LANES] = turned(k, cosine[...], sine[...]).astype(BF16)
    fresh[:, LANES:] = jnp.dot(normed, wv[...], preferred_element_type=F32).astype(BF16)
    step = 512
    count = held.shape[0]

    def body(b, _):
        base = pl.multiple_of(b * step, step)
        rows = lax.broadcasted_iota(jnp.int32, (step, count), 0) + base
        hit = (rows == index[...]).astype(F32)
        placed = jnp.dot(hit.astype(BF16), fresh[...], preferred_element_type=F32)
        taken = jnp.max(hit, axis=1, keepdims=True) > 0.0
        at = pl.ds(base, step)
        kk = jnp.where(taken, placed[:, :LANES], ck[at, :].astype(F32))
        vv = jnp.where(taken, placed[:, LANES:], cv[at, :].astype(F32))
        row = lax.broadcasted_iota(jnp.int32, (step, LANES), 0) + base
        bias = jnp.where(row < length[0], 0.0, MASKED)
        for j in range(2):
            ka[j, at, :] = key_rows(kk, j, bias)
            va[j, at, :] = value_rows(vv, j)
        return 0

    lax.fori_loop(0, ck.shape[0] // step, body, 0)


def prep(length, held, gain, wk, wv, cosine, sine, index, ck, cv):
    cap = ck.shape[0]
    out = jax.ShapeDtypeStruct((2, cap, LANES), BF16)
    return pl.pallas_call(
        prep_kernel,
        out_shape=(out, out),
        in_specs=[SM] + [VM] * 9,
        out_specs=(VM, VM),
        scratch_shapes=[pltpu.VMEM((held.shape[0], 2 * LANES), BF16)],
        compiler_params=pltpu.CompilerParams(vmem_limit_bytes=40 << 20),
        cost_estimate=pl.CostEstimate(flops=3 * 10**9, bytes_accessed=8 << 20, transcendentals=0),
        name="prep",
    )(length, held, gain, wk, wv, cosine, sine, index, ck, cv)


def qkv_kernel(pieces, *refs):
    xs, (wq, wk, wv, cosine, sine, q, k, v, x) = refs[:pieces], refs[pieces:]
    rows = xs[0].shape[0]
    for i, piece in enumerate(xs):
        x[i * rows : (i + 1) * rows, :] = piece[...]
    c, s = cosine[...], sine[...]
    xv = x[...]
    for j in range(wq.shape[1] // 256):
        got = jnp.dot(xv, wq[:, j * 256 : (j + 1) * 256], preferred_element_type=F32)
        for t in range(2):
            at = slice(j * 256 + t * LANES, j * 256 + (t + 1) * LANES)
            q[:, at] = turned(got[:, t * LANES : (t + 1) * LANES], c, s).astype(BF16)
    k[...] = turned(jnp.dot(xv, wk[...], preferred_element_type=F32), c, s).astype(BF16)
    v[...] = jnp.dot(xv, wv[...], preferred_element_type=F32).astype(BF16)


def qkv(xs, wq, wk, wv, cosine, sine):
    rows = sum(x.shape[0] for x in xs)
    out = lambda n: jax.ShapeDtypeStruct((rows, n), BF16)
    return pl.pallas_call(
        functools.partial(qkv_kernel, len(xs)),
        out_shape=(out(wq.shape[1]), out(LANES), out(LANES)),
        in_specs=[VM] * (len(xs) + 5),
        out_specs=(VM,) * 3,
        scratch_shapes=[pltpu.VMEM((rows, xs[0].shape[1]), BF16)],
        compiler_params=pltpu.CompilerParams(vmem_limit_bytes=24 << 20),
        cost_estimate=pl.CostEstimate(
            flops=2 * rows * 2048 * 768, bytes_accessed=5 << 20, transcendentals=0
        ),
        name="qkv",
    )(*xs, wq, wk, wv, cosine, sine)


KEYS = 512
CHUNKS = 1


def att_kernel(portion, chunk, chunks, scal, q, ka, va, *refs):
    kn, vn = refs[:chunks], refs[chunks : 2 * chunks]
    o, qa, na, nv, acc, low = refs[2 * chunks :]
    tokens = q.shape[0]
    length, head = scal[0], scal[1]
    per = q.shape[1] // HD // 2
    rows = per * tokens
    blocks = lax.div(length + (KEYS - 1), KEYS)

    def token(i, part):
        which = lax.div(i, portion)
        return (which ^ head) * (portion * chunks) + part * portion + (i - which * portion)

    own = token(lax.broadcasted_iota(jnp.int32, (tokens, tokens), 0), chunk)
    allowed = [
        token(lax.broadcasted_iota(jnp.int32, (tokens, tokens), 1), part) <= own
        for part in range(chunks)
    ]
    lane = lane_of((tokens, LANES))
    for j in range(2):
        for part in range(chunks):
            na[part] = key_rows(kn[part][...].astype(F32), j, 0.0)
            nv[part] = value_rows(vn[part][...].astype(F32), j)

        def put_queries(g, offset):
            pair = (j * per + g) // 2
            x = q[:, pair * LANES : (pair + 1) * LANES].astype(F32)
            tail = jnp.where(lane == HD, offset, jnp.where(lane == HD + 1, 1.0, 0.0))
            qa[g * tokens : (g + 1) * tokens, :] = jnp.where(
                lane < HD, head_lanes(x, g % 2), tail
            ).astype(BF16)

        for g in range(per):
            put_queries(g, 0.0)
            at = slice(g * tokens, (g + 1) * tokens)
            first = lax.dot_general(qa[at, :], ka[j, :256, :], NT, preferred_element_type=F32)
            put_queries(g, -jnp.max(first, axis=1, keepdims=True))

        def weights(keys, at):
            s = lax.dot_general(qa[at, :], keys, NT, preferred_element_type=F32)
            return jnp.exp2(s * FACTOR)

        for g in range(per):
            at = slice(g * tokens, (g + 1) * tokens)
            total = jnp.zeros((tokens, LANES), F32)
            for part in range(chunks):
                p = jnp.where(allowed[part], weights(na[part], at), 0.0)
                total += jnp.dot(p.astype(BF16), nv[part], preferred_element_type=F32)
            acc[at, :] = total

        def body(b, _):
            at = pl.ds(pl.multiple_of(b * KEYS, KEYS), KEYS)
            keys, values = ka[j, at, :], va[j, at, :]
            for g in range(per):
                q_at = slice(g * tokens, (g + 1) * tokens)
                p = weights(keys, q_at).astype(BF16)
                acc[q_at, :] += jnp.dot(p, values, preferred_element_type=F32)
            return 0

        lax.fori_loop(0, blocks, body, 0)

        safe = jnp.min((acc[:, HD : HD + 1] < TOP).astype(F32)) > 0.5

        @pl.when(jnp.logical_not(safe))
        def _():
            for g in range(per):
                put_queries(g, 0.0)
            acc[...] = jnp.zeros_like(acc)
            low[...] = jnp.full_like(low, MASKED)

            def take(keys, values, permitted, at):
                s = lax.dot_general(qa[at, :], keys, NT, preferred_element_type=F32)
                if permitted is not None:
                    s = jnp.where(permitted, s, MASKED)
                past = low[at, :]
                top = jnp.maximum(past, jnp.max(s, axis=1, keepdims=True))
                p = jnp.exp2((s - top[:, :1]) * FACTOR)
                shrink = jnp.exp2((past - top) * FACTOR)
                low[at, :] = top
                acc[at, :] = acc[at, :] * shrink + jnp.dot(
                    p.astype(BF16), values, preferred_element_type=F32
                )

            def redo(b, _):
                at = pl.ds(pl.multiple_of(b * KEYS, KEYS), KEYS)
                for g in range(per):
                    take(ka[j, at, :], va[j, at, :], None, slice(g * tokens, (g + 1) * tokens))
                return 0

            lax.fori_loop(0, blocks, redo, 0)
            for g in range(per):
                for part in range(chunks):
                    take(na[part], nv[part], allowed[part], slice(g * tokens, (g + 1) * tokens))

        for g in range(0, per, 2):
            pair = []
            for t in range(2):
                got = acc[(g + t) * tokens : (g + t + 1) * tokens, :]
                pair.append(got / got[:, HD : HD + 1])
            at = slice((j * per + g) * HD, (j * per + g + 2) * HD)
            o[:, at] = jnp.where(lane < HD, pair[0], pltpu.roll(pair[1], HD, 1)).astype(BF16)


def attend(portion, chunk, scal, q, ka, va, kns, vns):
    tokens, chunks = q.shape[0], len(kns)
    rows = q.shape[1] // HD // 2 * tokens
    return pl.pallas_call(
        functools.partial(att_kernel, portion, chunk, chunks),
        out_shape=jax.ShapeDtypeStruct(q.shape, BF16),
        in_specs=[SM] + [VM] * (3 + 2 * chunks),
        out_specs=VM,
        scratch_shapes=[
            pltpu.VMEM((rows, LANES), BF16),
            pltpu.VMEM((chunks, tokens, LANES), BF16),
            pltpu.VMEM((chunks, tokens, LANES), BF16),
            pltpu.VMEM((rows, LANES), F32),
            pltpu.VMEM((rows, LANES), F32),
        ],
        compiler_params=pltpu.CompilerParams(vmem_limit_bytes=40 << 20),
        cost_estimate=pl.CostEstimate(
            flops=4 * rows * 2 * 4608 * 128, bytes_accessed=6 << 20, transcendentals=rows * 2 * 4608
        ),
        name="attend",
    )(scal, q, ka, va, *kns, *vns)


def tables(positions):
    ladder = jnp.arange(HD // 2).astype(F32)
    frequency = jnp.exp(ladder * (-2.0 * math.log(ROPE_BASE) / HD))
    angles = positions[:, None] * frequency
    cosine, sine = jnp.cos(angles), jnp.sin(angles)
    return (
        jnp.concatenate([cosine] * 4, axis=-1),
        jnp.concatenate([-sine, sine, -sine, sine], axis=-1),
    )


def pick_kernel(order, x, out):
    for s in range(out.shape[0]):
        out[s] = x[order[s]]


def pick(x, order):
    return pl.pallas_call(
        pick_kernel,
        out_shape=jax.ShapeDtypeStruct(x.shape, x.dtype),
        in_specs=[SM, VM],
        out_specs=VM,
        name="pick",
    )(order, x)


def swap(x, axis, bits):
    size = lax.axis_size(axis)
    return lax.ppermute(x, axis, [(i, i ^ bits) for i in range(size)])


def spread(x):
    groups = lax.axis_size("req")
    rows, features = x.shape
    pieces = x.reshape(groups, rows // groups, features)
    return lax.all_to_all(pieces, "req", split_axis=0, concat_axis=0, tiled=True)


def shards(
    hidden_in,
    norm_gain,
    query_weight,
    key_weight,
    value_weight,
    output_weight,
    cache_keys,
    cache_values,
    held_states,
    cache_lengths,
    recompute_index,
    slot_request,
):
    requests_here, positions_here, features = hidden_in.shape
    assert requests_here == 1
    heads = lax.axis_size("head")
    head = lax.axis_index("head")
    portion = positions_here // CHUNKS
    mine = hidden_in[0]
    gain = norm_gain[None, :]
    normed = rms_scaled(mine.astype(F32), gain)
    length = cache_lengths[0]
    relative = jnp.arange(heads) ^ head
    tables_of = [
        tables(
            (
                relative[:, None] * positions_here + part * portion + jnp.arange(portion)[None, :]
            ).reshape(-1).astype(F32)
            + length.astype(F32)
        )
        for part in range(CHUNKS)
    ]
    scal = jnp.stack([length, head.astype(jnp.int32)])

    parts = [normed[c * portion : (c + 1) * portion] for c in range(CHUNKS)]
    spreads = [spread(x) for x in parts]
    slotted = [spread(pick(x, slot_request).reshape(portion, features)) for x in spreads]

    held_cos, held_sin = tables(recompute_index[0].astype(F32))
    ka, va = prep(
        cache_lengths,
        held_states[0],
        gain,
        key_weight,
        value_weight,
        held_cos,
        held_sin,
        recompute_index,
        cache_keys[0],
        cache_values[0],
    )

    qs, kns, vns = [], [], []
    for c in range(CHUNKS):
        own = slotted[c].reshape(portion, features)
        order = {0: own}
        step = heads // 2
        while step >= 1:
            for d in list(order):
                order[d | step] = swap(order[d], "head", step)
            step //= 2
        xs = [order[d] for d in range(heads)]
        q, kn, vn = qkv(xs, query_weight, key_weight, value_weight, *tables_of[c])
        qs.append(q)
        kns.append(kn)
        vns.append(vn)

    slots = jnp.arange(slot_request.shape[0], dtype=jnp.int32)
    inverse = jnp.sum(jnp.where(slot_request[None, :] == slots[:, None], slots[None, :], 0), axis=1)
    backs = []
    for c in range(CHUNKS):
        attended = attend(portion, c, scal, qs[c], ka, va, kns, vns)
        terms = jnp.dot(attended, output_weight, preferred_element_type=F32).astype(BF16)
        terms = terms.reshape(heads, portion, features)
        total = terms[0].astype(F32)
        for d in range(1, heads):
            total = total + swap(terms[d], "head", d).astype(F32)
        backs.append(spread(total.astype(BF16)))
    returned = [spread(pick(x, inverse).reshape(portion, features)) for x in backs]
    returned = jnp.concatenate([x.reshape(portion, features) for x in returned], axis=0)
    hidden_out = (mine.astype(F32) + returned.astype(F32)).astype(BF16)

    def by_token(pieces):
        stacked = jnp.stack([x.reshape(heads, portion, LANES) for x in pieces], axis=1)
        return jnp.take(stacked, relative, axis=0).reshape(1, heads * positions_here, LANES)

    return (hidden_out[None], by_token(kns), by_token(vns))


def solution(mesh):
    return jax.shard_map(
        shards,
        mesh=mesh,
        in_specs=(
            P("req", "head", None),
            P(),
            P(None, "head"),
            P(None, "head"),
            P(None, "head"),
            P("head", None),
            P("req", None, "head"),
            P("req", None, "head"),
            P("req", None, None),
            P("req"),
            P("req", None),
            P(),
        ),
        out_specs=(P("req", "head", None), P("req", None, "head"), P("req", None, "head")),
        check_vma=False,
    )
```

```python
import functools, math
import jax
import jax.numpy as jnp
from jax import lax
from jax.experimental import pallas as pl
from jax.experimental.pallas import tpu as pltpu
from jax.sharding import PartitionSpec as P

HD = 64
LANES = 128
F32 = jnp.float32
BF16 = jnp.bfloat16
ROPE_BASE = 500000.0
MASKED = -1e30
TOP = 2.0**100
FACTOR = HD**-0.5 * math.log2(math.e)
NT = (((1,), (1,)), ((), ()))
VM = pl.BlockSpec(memory_space=pltpu.VMEM)
SM = pl.BlockSpec(memory_space=pltpu.SMEM)


def hbm(x):
    return pltpu.with_memory_space_constraint(x, pltpu.HBM)


def rms_scaled(values, gains):
    factor = lax.rsqrt(jnp.mean(values * values, axis=-1, keepdims=True) + 1e-05)
    return (values * factor * gains).astype(BF16)


def lane_of(shape):
    return lax.broadcasted_iota(jnp.int32, shape, len(shape) - 1)


def turned(x, cosine, sine):
    lane = lane_of(x.shape)
    swapped = jnp.where(
        lane % HD < HD // 2, pltpu.roll(x, LANES - HD // 2, 1), pltpu.roll(x, HD // 2, 1)
    )
    return x * cosine + swapped * sine


def head_lanes(x, which):
    return x if which == 0 else pltpu.roll(x, HD, 1)


def key_rows(k, which, bias):
    lane = lane_of(k.shape)
    tail = jnp.where(lane == HD, 1.0, jnp.where(lane == HD + 1, bias, 0.0))
    return jnp.where(lane < HD, head_lanes(k, which), tail).astype(BF16)


def value_rows(v, which):
    lane = lane_of(v.shape)
    return jnp.where(lane < HD, head_lanes(v, which), jnp.where(lane == HD, 1.0, 0.0)).astype(BF16)


def prep_kernel(length, held, gain, wk, wv, cosine, sine, index, ck, cv, ka, va, fresh):
    normed = rms_scaled(held[...].astype(F32), gain[...])
    k = jnp.dot(normed, wk[...], preferred_element_type=F32)
    fresh[:, :LANES] = turned(k, cosine[...], sine[...]).astype(BF16)
    fresh[:, LANES:] = jnp.dot(normed, wv[...], preferred_element_type=F32).astype(BF16)
    step = 512
    count = held.shape[0]

    def body(b, _):
        base = pl.multiple_of(b * step, step)
        rows = lax.broadcasted_iota(jnp.int32, (step, count), 0) + base
        hit = (rows == index[...]).astype(F32)
        placed = jnp.dot(hit.astype(BF16), fresh[...], preferred_element_type=F32)
        taken = jnp.max(hit, axis=1, keepdims=True) > 0.0
        at = pl.ds(base, step)
        kk = jnp.where(taken, placed[:, :LANES], ck[at, :].astype(F32))
        vv = jnp.where(taken, placed[:, LANES:], cv[at, :].astype(F32))
        row = lax.broadcasted_iota(jnp.int32, (step, LANES), 0) + base
        bias = jnp.where(row < length[0], 0.0, MASKED)
        for j in range(2):
            ka[j, at, :] = key_rows(kk, j, bias)
            va[j, at, :] = value_rows(vv, j)
        return 0

    lax.fori_loop(0, ck.shape[0] // step, body, 0)


def prep(length, held, gain, wk, wv, cosine, sine, index, ck, cv):
    cap = ck.shape[0]
    out = jax.ShapeDtypeStruct((2, cap, LANES), BF16)
    return pl.pallas_call(
        prep_kernel,
        out_shape=(out, out),
        in_specs=[SM] + [VM] * 9,
        out_specs=(VM, VM),
        scratch_shapes=[pltpu.VMEM((held.shape[0], 2 * LANES), BF16)],
        compiler_params=pltpu.CompilerParams(vmem_limit_bytes=40 << 20),
        cost_estimate=pl.CostEstimate(flops=3 * 10**9, bytes_accessed=8 << 20, transcendentals=0),
        name="prep",
    )(length, held, gain, wk, wv, cosine, sine, index, ck, cv)


def qkv_kernel(pieces, *refs):
    xs, (wq, wk, wv, cosine, sine, q, k, v, x, bq, bk, bv, done) = refs[:pieces], refs[pieces:]
    rows = xs[0].shape[0]
    copies = [
        pltpu.make_async_copy(piece, x.at[i * rows : (i + 1) * rows, :], done.at[i])
        for i, piece in enumerate(xs)
    ]
    for i, (w, buffer) in enumerate(((wk, bk), (wv, bv), (wq, bq))):
        copies.append(pltpu.make_async_copy(w, buffer, done.at[pieces + i]))
    for copy in copies:
        copy.start()
    c, s = cosine[...], sine[...]
    for copy in copies[: pieces + 1]:
        copy.wait()
    xv = x[...]
    k[...] = turned(jnp.dot(xv, bk[...], preferred_element_type=F32), c, s).astype(BF16)
    copies[pieces + 1].wait()
    v[...] = jnp.dot(xv, bv[...], preferred_element_type=F32).astype(BF16)
    copies[pieces + 2].wait()
    for j in range(wq.shape[1] // 256):
        got = jnp.dot(xv, bq[:, j * 256 : (j + 1) * 256], preferred_element_type=F32)
        for t in range(2):
            at = slice(j * 256 + t * LANES, j * 256 + (t + 1) * LANES)
            q[:, at] = turned(got[:, t * LANES : (t + 1) * LANES], c, s).astype(BF16)


def qkv(xs, wq, wk, wv, cosine, sine):
    rows = sum(x.shape[0] for x in xs)
    depth, width = wq.shape
    out = lambda n: jax.ShapeDtypeStruct((rows, n), BF16)
    raw = pl.BlockSpec(memory_space=pltpu.HBM)
    any_place = pl.BlockSpec(memory_space=pl.ANY)
    return pl.pallas_call(
        functools.partial(qkv_kernel, len(xs)),
        out_shape=(out(width), out(LANES), out(LANES)),
        in_specs=[any_place] * len(xs) + [raw] * 3 + [VM] * 2,
        out_specs=(VM,) * 3,
        scratch_shapes=[
            pltpu.VMEM((rows, depth), BF16),
            pltpu.VMEM((depth, width), BF16),
            pltpu.VMEM((depth, LANES), BF16),
            pltpu.VMEM((depth, LANES), BF16),
            pltpu.SemaphoreType.DMA((len(xs) + 3,)),
        ],
        compiler_params=pltpu.CompilerParams(vmem_limit_bytes=16 << 20),
        cost_estimate=pl.CostEstimate(
            flops=2 * rows * depth * (width + 2 * LANES), bytes_accessed=5 << 20, transcendentals=0
        ),
        name="qkv",
    )(*xs, hbm(wq), hbm(wk), hbm(wv), cosine, sine)


KEYS = 1024
ROWS = 1024
CHUNKS = 1


def att_kernel(portion, chunk, chunks, js, mode, scal, q, ka, va, *refs):
    refs = list(refs)
    take_refs = lambda count: [refs.pop(0) for _ in range(count)]
    if mode != "cached":
        kn, vn = take_refs(chunks), take_refs(chunks)
    if mode == "new":
        qa_in, acc_in = take_refs(2)
    if mode == "cached":
        qa_out, acc_out = take_refs(2)
    else:
        (o,) = take_refs(1)
    if mode != "cached":
        qa_s, acc_s, na, nv, low = take_refs(5)
    if mode == "new":
        kbuf, vbuf = take_refs(2)
    tokens = q.shape[0]
    length, head = scal[0], scal[1]
    per = q.shape[1] // HD // 2
    rows = per * tokens
    blocks = lax.div(length + (KEYS - 1), KEYS)
    lane = lane_of((tokens, LANES))
    spans = [slice(g * tokens, (g + 1) * tokens) for g in range(per)]

    def token(i, part):
        which = lax.div(i, portion)
        swapped = which if mode is None else lax.div(which, 2) + 2 * lax.rem(which, 2)
        return (swapped ^ head) * (portion * chunks) + part * portion + (i - which * portion)

    if mode != "cached":
        own = token(lax.broadcasted_iota(jnp.int32, (tokens, tokens), 0), chunk)
        allowed = [
            token(lax.broadcasted_iota(jnp.int32, (tokens, tokens), 1), part) <= own
            for part in range(chunks)
        ]

    for n, j in enumerate(js):
        if mode == "cached":
            qa, acc = qa_out.at[n], acc_out.at[n]
        else:
            qa, acc = qa_s, acc_s

        def put_queries(g, offset):
            pair = (j * per + g) // 2
            x = q[:, pair * LANES : (pair + 1) * LANES].astype(F32)
            tail = jnp.where(lane == HD, offset, jnp.where(lane == HD + 1, 1.0, 0.0))
            qa[spans[g], :] = jnp.where(lane < HD, head_lanes(x, g % 2), tail).astype(BF16)

        def weights(keys, at):
            s = lax.dot_general(qa[at, :], keys, NT, preferred_element_type=F32)
            return jnp.exp2(s * FACTOR)

        if mode == "new":
            qa[...] = qa_in[n]
            acc[...] = acc_in[n]
        else:
            for g in range(per):
                put_queries(g, 0.0)
                first = lax.dot_general(
                    qa[spans[g], :], ka[j, :256, :], NT, preferred_element_type=F32
                )
                put_queries(g, -jnp.max(first, axis=1, keepdims=True))
            acc[...] = jnp.zeros(acc.shape, F32)

        if mode != "cached":
            for part in range(chunks):
                na[part] = key_rows(kn[part][...].astype(F32), j, 0.0)
                nv[part] = value_rows(vn[part][...].astype(F32), j)
            for g in range(per):
                total = acc[spans[g], :]
                for part in range(chunks):
                    p = jnp.where(allowed[part], weights(na[part], spans[g]), 0.0)
                    total += jnp.dot(p.astype(BF16), nv[part], preferred_element_type=F32)
                acc[spans[g], :] = total

        if mode != "new":

            def body(b, _):
                at = pl.ds(pl.multiple_of(b * KEYS, KEYS), KEYS)
                keys, values = ka[j, at, :], va[j, at, :]
                for r in range(rows // ROWS):
                    q_at = slice(r * ROWS, (r + 1) * ROWS)
                    p = weights(keys, q_at).astype(BF16)
                    acc[q_at, :] += jnp.dot(p, values, preferred_element_type=F32)
                return 0

            lax.fori_loop(0, blocks, body, 0)

        if mode == "cached":
            continue

        safe = jnp.min((acc[:, HD : HD + 1] < TOP).astype(F32)) > 0.5

        @pl.when(jnp.logical_not(safe))
        def _():
            if mode == "new":
                pltpu.sync_copy(ka.at[j], kbuf)
                pltpu.sync_copy(va.at[j], vbuf)
                old_k, old_v = kbuf, vbuf
            else:
                old_k, old_v = ka.at[j], va.at[j]
            for g in range(per):
                put_queries(g, 0.0)
            acc[...] = jnp.zeros(acc.shape, F32)
            low[...] = jnp.full(low.shape, MASKED, F32)

            def take(keys, values, permitted, at):
                s = lax.dot_general(qa[at, :], keys, NT, preferred_element_type=F32)
                if permitted is not None:
                    s = jnp.where(permitted, s, MASKED)
                past = low[at, :]
                top = jnp.maximum(past, jnp.max(s, axis=1, keepdims=True))
                p = jnp.exp2((s - top[:, :1]) * FACTOR)
                shrink = jnp.exp2((past - top) * FACTOR)
                low[at, :] = top
                acc[at, :] = acc[at, :] * shrink + jnp.dot(
                    p.astype(BF16), values, preferred_element_type=F32
                )

            def redo(b, _):
                at = pl.ds(pl.multiple_of(b * 512, 512), 512)
                for g in range(per):
                    take(old_k[at, :], old_v[at, :], None, spans[g])
                return 0

            lax.fori_loop(0, lax.div(length + 511, 512), redo, 0)
            for g in range(per):
                for part in range(chunks):
                    take(na[part], nv[part], allowed[part], spans[g])

        for g in range(0, per, 2):
            pair = []
            for t in range(2):
                got = acc[spans[g + t], :]
                pair.append(got / got[:, HD : HD + 1])
            at = slice((n * per + g) * HD, (n * per + g + 2) * HD)
            o[:, at] = jnp.where(lane < HD, pair[0], pltpu.roll(pair[1], HD, 1)).astype(BF16)


def attend(portion, chunk, js, mode, scal, q, ka, va, kns=(), vns=(), began=()):
    tokens, chunks = q.shape[0], CHUNKS
    rows = q.shape[1] // HD // 2 * tokens
    keys = {"cached": ka.shape[1], "new": tokens * chunks, "full": ka.shape[1] + tokens * chunks}[mode]
    scratch = []
    if mode != "cached":
        scratch = [
            pltpu.VMEM((rows, LANES), BF16),
            pltpu.VMEM((rows, LANES), F32),
            pltpu.VMEM((chunks, tokens, LANES), BF16),
            pltpu.VMEM((chunks, tokens, LANES), BF16),
            pltpu.VMEM((rows, LANES), F32),
        ]
    cached = VM
    if mode == "new":
        scratch += [pltpu.VMEM(ka.shape[1:], BF16)] * 2
        cached = pl.BlockSpec(memory_space=pl.ANY)
    if mode == "cached":
        shape = (len(js), rows, LANES)
        out = (jax.ShapeDtypeStruct(shape, BF16), jax.ShapeDtypeStruct(shape, F32))
        specs = (VM, VM)
    else:
        out = jax.ShapeDtypeStruct((tokens, q.shape[1] // 2 * len(js)), BF16)
        specs = VM
    return pl.pallas_call(
        functools.partial(att_kernel, portion, chunk, chunks, js, mode),
        out_shape=out,
        in_specs=[SM, VM, cached, cached] + [VM] * (len(kns) + len(vns) + len(began)),
        out_specs=specs,
        scratch_shapes=scratch,
        compiler_params=pltpu.CompilerParams(vmem_limit_bytes=32 << 20),
        cost_estimate=pl.CostEstimate(
            flops=4 * rows * len(js) * keys * 256,
            bytes_accessed=4 << 20,
            transcendentals=rows * len(js) * keys,
        ),
        name="attend_" + mode,
    )(scal, q, ka, va, *kns, *vns, *began)


def tables(positions):
    ladder = jnp.arange(HD // 2).astype(F32)
    frequency = jnp.exp(ladder * (-2.0 * math.log(ROPE_BASE) / HD))
    angles = positions[:, None] * frequency
    cosine, sine = jnp.cos(angles), jnp.sin(angles)
    return (
        jnp.concatenate([cosine] * 4, axis=-1),
        jnp.concatenate([-sine, sine, -sine, sine], axis=-1),
    )


def pick_kernel(order, x, out, done):
    count = out.shape[0]
    copies = [pltpu.make_async_copy(x.at[order[s]], out.at[s], done.at[s]) for s in range(count)]
    for copy in copies:
        copy.start()
    for copy in copies:
        copy.wait()


def pick(x, order):
    return pl.pallas_call(
        pick_kernel,
        out_shape=jax.ShapeDtypeStruct(x.shape, x.dtype),
        in_specs=[SM, pl.BlockSpec(memory_space=pl.ANY)],
        out_specs=pl.BlockSpec(memory_space=pl.ANY),
        scratch_shapes=[pltpu.SemaphoreType.DMA((x.shape[0],))],
        compiler_params=pltpu.CompilerParams(vmem_limit_bytes=1 << 20),
        name="pick",
    )(order, x)


def pick_norm_kernel(order, x, gain, out):
    for s in range(out.shape[0]):
        out[s] = rms_scaled(x[order[s]].astype(F32), gain[...])


def pick_norm(x, order, gain):
    return pl.pallas_call(
        pick_norm_kernel,
        out_shape=jax.ShapeDtypeStruct(x.shape, x.dtype),
        in_specs=[SM, VM, VM],
        out_specs=VM,
        compiler_params=pltpu.CompilerParams(vmem_limit_bytes=8 << 20),
        name="pick_norm",
    )(order, x, gain)


def project_kernel(mine, theirs, w, w_pair, keep, send):
    terms = [
        jnp.dot(x[...], y[...], preferred_element_type=F32).astype(BF16).astype(F32)
        for x, y in ((mine, w), (theirs, w_pair))
    ]
    total = terms[0] + terms[1]
    half = keep.shape[0]
    keep[...] = total[:half]
    send[...] = total[half:].astype(BF16)


def project(mine, theirs, w, w_pair):
    rows, depth = mine.shape
    width = w.shape[1]
    step = 512
    half = rows // 2
    return pl.pallas_call(
        project_kernel,
        out_shape=(
            jax.ShapeDtypeStruct((half, width), F32),
            jax.ShapeDtypeStruct((half, width), BF16),
        ),
        grid=(width // step,),
        in_specs=[pl.BlockSpec((rows, depth), lambda n: (0, 0))] * 2
        + [pl.BlockSpec((depth, step), lambda n: (0, n))] * 2,
        out_specs=(pl.BlockSpec((half, step), lambda n: (0, n)),) * 2,
        compiler_params=pltpu.CompilerParams(vmem_limit_bytes=16 << 20),
        cost_estimate=pl.CostEstimate(
            flops=4 * rows * depth * width, bytes_accessed=6 << 20, transcendentals=0
        ),
        name="project",
    )(mine, theirs, w, w_pair)


def swap(x, axis, bits):
    size = lax.axis_size(axis)
    return lax.ppermute(x, axis, [(i, i ^ bits) for i in range(size)])


def spread(x):
    groups = lax.axis_size("req")
    rows, features = x.shape
    pieces = x.reshape(groups, rows // groups, features)
    return lax.all_to_all(pieces, "req", split_axis=0, concat_axis=0, tiled=True)


def shards(
    hidden_in,
    norm_gain,
    query_weight,
    key_weight,
    value_weight,
    output_weight,
    cache_keys,
    cache_values,
    held_states,
    cache_lengths,
    recompute_index,
    slot_request,
):
    requests_here, positions_here, features = hidden_in.shape
    assert requests_here == 1
    heads = lax.axis_size("head")
    head = lax.axis_index("head")
    portion = positions_here // CHUNKS
    mine = hidden_in[0]
    gain = norm_gain[None, :]
    length = cache_lengths[0]
    relative = jnp.arange(heads).reshape(2, heads // 2).T.reshape(-1) ^ head
    tables_of = [
        tables(
            (
                relative[:, None] * positions_here + part * portion + jnp.arange(portion)[None, :]
            ).reshape(-1).astype(F32)
            + length.astype(F32)
        )
        for part in range(CHUNKS)
    ]
    scal = jnp.stack([length, head.astype(jnp.int32)])
    tie = lax.optimization_barrier
    flat = lambda x: x.reshape(portion, features)
    far_bit, near_bit = heads // 2, 1
    w_pair = swap(output_weight, "head", near_bit)
    held_cos, held_sin = tables(recompute_index[0].astype(F32))

    def project_in(c, own):
        far = swap(own, "head", far_bit)
        near = swap(own, "head", near_bit)
        corner = swap(far, "head", near_bit)
        return qkv([own, far, near, corner], query_weight, key_weight, value_weight, *tables_of[c])

    def project_out(pieces):
        attended = pieces[0] if len(pieces) == 1 else jnp.concatenate(pieces, axis=1)
        theirs = swap(attended[2 * portion :], "head", near_bit)
        keep, send = project(attended[: 2 * portion], theirs, output_weight, w_pair)
        return keep, swap(send, "head", far_bit)

    join = lambda keep, got: (keep + got.astype(F32)).astype(BF16)
    slots = jnp.arange(slot_request.shape[0], dtype=jnp.int32)
    inverse = jnp.sum(jnp.where(slot_request[None, :] == slots[:, None], slots[None, :], 0), axis=1)

    ka, va = prep(
        cache_lengths,
        held_states[0],
        gain,
        key_weight,
        value_weight,
        held_cos,
        held_sin,
        recompute_index,
        cache_keys[0],
        cache_values[0],
    )
    first = spread(mine)
    first, ka, va, tables_of = tie((first, ka, va, tables_of))
    own = flat(spread(flat(pick_norm(first, slot_request, gain))))
    q, kn, vn = project_in(0, own)
    kns, vns = [kn], [vn]
    attended = attend(portion, 0, (0, 1), "full", scal, q, ka, va, kns, vns)
    back = spread(join(*project_out([attended])))
    returned = [flat(spread(flat(pick(back, inverse))))]
    returned = jnp.concatenate(returned, axis=0)
    hidden_out = (mine.astype(F32) + returned.astype(F32)).astype(BF16)

    away = jnp.arange(heads) ^ head

    def by_token(pieces):
        stacked = jnp.stack([x.reshape(heads, portion, LANES) for x in pieces], axis=1)
        return jnp.take(stacked, lax.div(away, 2) + 2 * lax.rem(away, 2), axis=0).reshape(1, heads * positions_here, LANES)

    return (hidden_out[None], by_token(kns), by_token(vns))


def solution(mesh):
    return jax.shard_map(
        shards,
        mesh=mesh,
        in_specs=(
            P("req", "head", None),
            P(),
            P(None, "head"),
            P(None, "head"),
            P(None, "head"),
            P("head", None),
            P("req", None, "head"),
            P("req", None, "head"),
            P("req", None, None),
            P("req"),
            P("req", None),
            P(),
        ),
        out_specs=(P("req", "head", None), P("req", None, "head"), P("req", None, "head")),
        check_vma=False,
    )
```

```python
import functools, math
import jax
import jax.numpy as jnp
from jax import lax
from jax.experimental import pallas as pl
from jax.experimental.pallas import tpu as pltpu
from jax.sharding import PartitionSpec as P

HD = 64
LANES = 128
F32 = jnp.float32
BF16 = jnp.bfloat16
ROPE_BASE = 500000.0
MASKED = -1e30
TOP = 2.0**100
FACTOR = HD**-0.5 * math.log2(math.e)
NT = (((1,), (1,)), ((), ()))
VM = pl.BlockSpec(memory_space=pltpu.VMEM)
SM = pl.BlockSpec(memory_space=pltpu.SMEM)


def hbm(x):
    return pltpu.with_memory_space_constraint(x, pltpu.HBM)


def rms_scaled(values, gains):
    factor = lax.rsqrt(jnp.mean(values * values, axis=-1, keepdims=True) + 1e-05)
    return (values * factor * gains).astype(BF16)


def lane_of(shape):
    return lax.broadcasted_iota(jnp.int32, shape, len(shape) - 1)


def turned(x, cosine, sine):
    lane = lane_of(x.shape)
    swapped = jnp.where(
        lane % HD < HD // 2, pltpu.roll(x, LANES - HD // 2, 1), pltpu.roll(x, HD // 2, 1)
    )
    return x * cosine + swapped * sine


def head_lanes(x, which):
    return x if which == 0 else pltpu.roll(x, HD, 1)


def key_rows(k, which, bias):
    lane = lane_of(k.shape)
    tail = jnp.where(lane == HD, 1.0, jnp.where(lane == HD + 1, bias, 0.0))
    return jnp.where(lane < HD, head_lanes(k, which), tail).astype(BF16)


def value_rows(v, which):
    lane = lane_of(v.shape)
    return jnp.where(lane < HD, head_lanes(v, which), jnp.where(lane == HD, 1.0, 0.0)).astype(BF16)


def prep_kernel(length, held, gain, wk, wv, cosine, sine, index, ck, cv, ka, va, fresh):
    normed = rms_scaled(held[...].astype(F32), gain[...])
    k = jnp.dot(normed, wk[...], preferred_element_type=F32)
    fresh[:, :LANES] = turned(k, cosine[...], sine[...]).astype(BF16)
    fresh[:, LANES:] = jnp.dot(normed, wv[...], preferred_element_type=F32).astype(BF16)
    step = 512
    count = held.shape[0]

    def body(b, _):
        base = pl.multiple_of(b * step, step)
        rows = lax.broadcasted_iota(jnp.int32, (step, count), 0) + base
        hit = (rows == index[...]).astype(F32)
        placed = jnp.dot(hit.astype(BF16), fresh[...], preferred_element_type=F32)
        taken = jnp.max(hit, axis=1, keepdims=True) > 0.0
        at = pl.ds(base, step)
        kk = jnp.where(taken, placed[:, :LANES], ck[at, :].astype(F32))
        vv = jnp.where(taken, placed[:, LANES:], cv[at, :].astype(F32))
        row = lax.broadcasted_iota(jnp.int32, (step, LANES), 0) + base
        bias = jnp.where(row < length[0], 0.0, MASKED)
        for j in range(2):
            ka[j, at, :] = key_rows(kk, j, bias)
            va[j, at, :] = value_rows(vv, j)
        return 0

    lax.fori_loop(0, ck.shape[0] // step, body, 0)


def prep(length, held, gain, wk, wv, cosine, sine, index, ck, cv):
    cap = ck.shape[0]
    out = jax.ShapeDtypeStruct((2, cap, LANES), BF16)
    return pl.pallas_call(
        prep_kernel,
        out_shape=(out, out),
        in_specs=[SM] + [VM] * 9,
        out_specs=(VM, VM),
        scratch_shapes=[pltpu.VMEM((held.shape[0], 2 * LANES), BF16)],
        compiler_params=pltpu.CompilerParams(vmem_limit_bytes=40 << 20),
        cost_estimate=pl.CostEstimate(flops=3 * 10**9, bytes_accessed=8 << 20, transcendentals=0),
        name="prep",
    )(length, held, gain, wk, wv, cosine, sine, index, ck, cv)


def qkv_kernel(pieces, *refs):
    xs, (wq, wk, wv, cosine, sine, q, k, v, x, bq, bk, bv, done) = refs[:pieces], refs[pieces:]
    rows = xs[0].shape[0]
    copies = [
        pltpu.make_async_copy(piece, x.at[i * rows : (i + 1) * rows, :], done.at[i])
        for i, piece in enumerate(xs)
    ]
    for i, (w, buffer) in enumerate(((wk, bk), (wv, bv), (wq, bq))):
        copies.append(pltpu.make_async_copy(w, buffer, done.at[pieces + i]))
    for copy in copies:
        copy.start()
    c, s = cosine[...], sine[...]
    for copy in copies[: pieces + 1]:
        copy.wait()
    xv = x[...]
    k[...] = turned(jnp.dot(xv, bk[...], preferred_element_type=F32), c, s).astype(BF16)
    copies[pieces + 1].wait()
    v[...] = jnp.dot(xv, bv[...], preferred_element_type=F32).astype(BF16)
    copies[pieces + 2].wait()
    for j in range(wq.shape[1] // 256):
        got = jnp.dot(xv, bq[:, j * 256 : (j + 1) * 256], preferred_element_type=F32)
        for t in range(2):
            at = slice(j * 256 + t * LANES, j * 256 + (t + 1) * LANES)
            q[:, at] = turned(got[:, t * LANES : (t + 1) * LANES], c, s).astype(BF16)


def qkv(xs, wq, wk, wv, cosine, sine):
    rows = sum(x.shape[0] for x in xs)
    depth, width = wq.shape
    out = lambda n: jax.ShapeDtypeStruct((rows, n), BF16)
    raw = pl.BlockSpec(memory_space=pltpu.HBM)
    any_place = pl.BlockSpec(memory_space=pl.ANY)
    return pl.pallas_call(
        functools.partial(qkv_kernel, len(xs)),
        out_shape=(out(width), out(LANES), out(LANES)),
        in_specs=[any_place] * len(xs) + [raw] * 3 + [VM] * 2,
        out_specs=(VM,) * 3,
        scratch_shapes=[
            pltpu.VMEM((rows, depth), BF16),
            pltpu.VMEM((depth, width), BF16),
            pltpu.VMEM((depth, LANES), BF16),
            pltpu.VMEM((depth, LANES), BF16),
            pltpu.SemaphoreType.DMA((len(xs) + 3,)),
        ],
        compiler_params=pltpu.CompilerParams(vmem_limit_bytes=16 << 20),
        cost_estimate=pl.CostEstimate(
            flops=2 * rows * depth * (width + 2 * LANES), bytes_accessed=5 << 20, transcendentals=0
        ),
        name="qkv",
    )(*xs, hbm(wq), hbm(wk), hbm(wv), cosine, sine)


KEYS = 1024
ROWS = 1024
PARTS = 2


def att_kernel(chunks, js, mode, scal, q, ka, va, *refs):
    refs = list(refs)
    take_refs = lambda count: [refs.pop(0) for _ in range(count)]
    if mode != "cached":
        kn, vn = take_refs(chunks), take_refs(chunks)
        (col,), row = take_refs(1), take_refs(chunks)
    if mode == "new":
        qa_in, acc_in = take_refs(2)
    if mode == "cached":
        qa_out, acc_out = take_refs(2)
    else:
        (o,) = take_refs(1)
    if mode != "cached":
        qa_s, acc_s, na, nv, low = take_refs(5)
    if mode == "new":
        kbuf, vbuf = take_refs(2)
    tokens = q.shape[0]
    length = scal[0]
    per = q.shape[1] // HD // 2
    rows = per * tokens
    blocks = lax.div(length + (KEYS - 1), KEYS)
    lane = lane_of((tokens, LANES))
    spans = [slice(g * tokens, (g + 1) * tokens) for g in range(per)]

    if mode != "cached":
        allowed = [jnp.broadcast_to(x[...], (tokens, tokens)) <= col[...] for x in row]

    for n, j in enumerate(js):
        if mode == "cached":
            qa, acc = qa_out.at[n], acc_out.at[n]
        else:
            qa, acc = qa_s, acc_s

        def put_queries(g, offset):
            pair = (j * per + g) // 2
            x = q[:, pair * LANES : (pair + 1) * LANES].astype(F32)
            tail = jnp.where(lane == HD, offset, jnp.where(lane == HD + 1, 1.0, 0.0))
            qa[spans[g], :] = jnp.where(lane < HD, head_lanes(x, g % 2), tail).astype(BF16)

        def weights(keys, at):
            s = lax.dot_general(qa[at, :], keys, NT, preferred_element_type=F32)
            return jnp.exp2(s * FACTOR)

        if mode == "new":
            qa[...] = qa_in[n]
            acc[...] = acc_in[n]
        else:
            for g in range(per):
                put_queries(g, 0.0)
                first = lax.dot_general(
                    qa[spans[g], :], ka[j, :256, :], NT, preferred_element_type=F32
                )
                put_queries(g, -jnp.max(first, axis=1, keepdims=True))
            acc[...] = jnp.zeros(acc.shape, F32)

        if mode != "cached":
            for part in range(chunks):
                na[part] = key_rows(kn[part][...].astype(F32), j, 0.0)
                nv[part] = value_rows(vn[part][...].astype(F32), j)
            for g in range(per):
                total = acc[spans[g], :]
                for part in range(chunks):
                    p = jnp.where(allowed[part], weights(na[part], spans[g]), 0.0)
                    total += jnp.dot(p.astype(BF16), nv[part], preferred_element_type=F32)
                acc[spans[g], :] = total

        if mode != "new":

            def body(b, _):
                at = pl.ds(pl.multiple_of(b * KEYS, KEYS), KEYS)
                keys, values = ka[j, at, :], va[j, at, :]
                for r in range(rows // ROWS):
                    q_at = slice(r * ROWS, (r + 1) * ROWS)
                    p = weights(keys, q_at).astype(BF16)
                    acc[q_at, :] += jnp.dot(p, values, preferred_element_type=F32)
                return 0

            lax.fori_loop(0, blocks, body, 0)

        if mode == "cached":
            continue

        safe = jnp.min((acc[:, HD : HD + 1] < TOP).astype(F32)) > 0.5

        @pl.when(jnp.logical_not(safe))
        def _():
            if mode == "new":
                pltpu.sync_copy(ka.at[j], kbuf)
                pltpu.sync_copy(va.at[j], vbuf)
                old_k, old_v = kbuf, vbuf
            else:
                old_k, old_v = ka.at[j], va.at[j]
            for g in range(per):
                put_queries(g, 0.0)
            acc[...] = jnp.zeros(acc.shape, F32)
            low[...] = jnp.full(low.shape, MASKED, F32)

            def take(keys, values, permitted, at):
                s = lax.dot_general(qa[at, :], keys, NT, preferred_element_type=F32)
                if permitted is not None:
                    s = jnp.where(permitted, s, MASKED)
                past = low[at, :]
                top = jnp.maximum(past, jnp.max(s, axis=1, keepdims=True))
                p = jnp.exp2((s - top[:, :1]) * FACTOR)
                shrink = jnp.exp2((past - top) * FACTOR)
                low[at, :] = top
                acc[at, :] = acc[at, :] * shrink + jnp.dot(
                    p.astype(BF16), values, preferred_element_type=F32
                )

            def redo(b, _):
                at = pl.ds(pl.multiple_of(b * 512, 512), 512)
                for g in range(per):
                    take(old_k[at, :], old_v[at, :], None, spans[g])
                return 0

            lax.fori_loop(0, lax.div(length + 511, 512), redo, 0)
            for g in range(per):
                for part in range(chunks):
                    take(na[part], nv[part], allowed[part], spans[g])

        for g in range(0, per, 2):
            pair = []
            for t in range(2):
                got = acc[spans[g + t], :]
                pair.append(got / got[:, HD : HD + 1])
            at = slice((n * per + g) * HD, (n * per + g + 2) * HD)
            o[:, at] = jnp.where(lane < HD, pair[0], pltpu.roll(pair[1], HD, 1)).astype(BF16)


def attend(js, mode, scal, q, ka, va, kns=(), vns=(), places=(), began=()):
    tokens, chunks = q.shape[0], PARTS
    rows = q.shape[1] // HD // 2 * tokens
    keys = {"cached": ka.shape[1], "new": tokens * chunks, "full": ka.shape[1] + tokens * chunks}[mode]
    scratch = []
    if mode != "cached":
        scratch = [
            pltpu.VMEM((rows, LANES), BF16),
            pltpu.VMEM((rows, LANES), F32),
            pltpu.VMEM((chunks, tokens, LANES), BF16),
            pltpu.VMEM((chunks, tokens, LANES), BF16),
            pltpu.VMEM((rows, LANES), F32),
        ]
    cached = VM
    if mode == "new":
        scratch += [pltpu.VMEM(ka.shape[1:], BF16)] * 2
        cached = pl.BlockSpec(memory_space=pl.ANY)
    if mode == "cached":
        shape = (len(js), rows, LANES)
        out = (jax.ShapeDtypeStruct(shape, BF16), jax.ShapeDtypeStruct(shape, F32))
        specs = (VM, VM)
    else:
        out = jax.ShapeDtypeStruct((tokens, q.shape[1] // 2 * len(js)), BF16)
        specs = VM
    return pl.pallas_call(
        functools.partial(att_kernel, chunks, js, mode),
        out_shape=out,
        in_specs=[SM, VM, cached, cached] + [VM] * (len(kns) + len(vns) + len(places) + len(began)),
        out_specs=specs,
        scratch_shapes=scratch,
        compiler_params=pltpu.CompilerParams(vmem_limit_bytes=32 << 20),
        cost_estimate=pl.CostEstimate(
            flops=4 * rows * len(js) * keys * 256,
            bytes_accessed=4 << 20,
            transcendentals=rows * len(js) * keys,
        ),
        name="attend_" + mode,
    )(scal, q, ka, va, *kns, *vns, *places, *began)


def tables(positions):
    ladder = jnp.arange(HD // 2).astype(F32)
    frequency = jnp.exp(ladder * (-2.0 * math.log(ROPE_BASE) / HD))
    angles = positions[:, None] * frequency
    cosine, sine = jnp.cos(angles), jnp.sin(angles)
    return (
        jnp.concatenate([cosine] * 4, axis=-1),
        jnp.concatenate([-sine, sine, -sine, sine], axis=-1),
    )


def pick_kernel(order, x, out, done):
    count = out.shape[0]
    copies = [pltpu.make_async_copy(x.at[order[s]], out.at[s], done.at[s]) for s in range(count)]
    for copy in copies:
        copy.start()
    for copy in copies:
        copy.wait()


def pick(x, order):
    return pl.pallas_call(
        pick_kernel,
        out_shape=jax.ShapeDtypeStruct(x.shape, x.dtype),
        in_specs=[SM, pl.BlockSpec(memory_space=pl.ANY)],
        out_specs=pl.BlockSpec(memory_space=pl.ANY),
        scratch_shapes=[pltpu.SemaphoreType.DMA((x.shape[0],))],
        compiler_params=pltpu.CompilerParams(vmem_limit_bytes=1 << 20),
        name="pick",
    )(order, x)


def pick_norm_kernel(order, x, gain, out):
    for s in range(out.shape[0]):
        out[s] = rms_scaled(x[order[s]].astype(F32), gain[...])


def pick_norm(x, order, gain):
    return pl.pallas_call(
        pick_norm_kernel,
        out_shape=jax.ShapeDtypeStruct(x.shape, x.dtype),
        in_specs=[SM, VM, VM],
        out_specs=VM,
        compiler_params=pltpu.CompilerParams(vmem_limit_bytes=8 << 20),
        name="pick_norm",
    )(order, x, gain)


def project_kernel(mine, theirs, w, w_pair, out):
    terms = [
        jnp.dot(x[...], y[...], preferred_element_type=F32).astype(BF16).astype(F32)
        for x, y in ((mine, w), (theirs, w_pair))
    ]
    out[...] = (terms[0] + terms[1]).astype(out.dtype)


def project(mine, theirs, w, w_pair, kind):
    rows, depth = mine.shape
    width = w.shape[1]
    step = 512
    return pl.pallas_call(
        project_kernel,
        out_shape=jax.ShapeDtypeStruct((rows, width), kind),
        grid=(width // step,),
        in_specs=[pl.BlockSpec((rows, depth), lambda n: (0, 0))] * 2
        + [pl.BlockSpec((depth, step), lambda n: (0, n))] * 2,
        out_specs=pl.BlockSpec((rows, step), lambda n: (0, n)),
        compiler_params=pltpu.CompilerParams(vmem_limit_bytes=16 << 20),
        cost_estimate=pl.CostEstimate(
            flops=4 * rows * depth * width, bytes_accessed=6 << 20, transcendentals=0
        ),
        name="project",
    )(mine, theirs, w, w_pair)


def swap(x, axis, bits):
    size = lax.axis_size(axis)
    return lax.ppermute(x, axis, [(i, i ^ bits) for i in range(size)])


def spread(x):
    groups = lax.axis_size("req")
    rows, features = x.shape
    pieces = x.reshape(groups, rows // groups, features)
    return lax.all_to_all(pieces, "req", split_axis=0, concat_axis=0, tiled=True)


def shards(
    hidden_in,
    norm_gain,
    query_weight,
    key_weight,
    value_weight,
    output_weight,
    cache_keys,
    cache_values,
    held_states,
    cache_lengths,
    recompute_index,
    slot_request,
):
    requests_here, positions_here, features = hidden_in.shape
    assert requests_here == 1
    heads = lax.axis_size("head")
    head = lax.axis_index("head")
    mine = hidden_in[0]
    gain = norm_gain[None, :]
    length = cache_lengths[0]
    tie = lax.optimization_barrier
    flat = lambda x: x.reshape(positions_here, features)
    far_bit, near_bit = heads // 2, 1
    inner = jnp.arange(positions_here)
    place = lambda bits: jnp.concatenate(
        [(head ^ bit) * positions_here + inner for bit in bits]
    ).astype(jnp.int32)
    here, there = place((0, near_bit)), place((far_bit, far_bit + near_bit))
    new_tables = [tables(length.astype(F32) + x.astype(F32)) for x in (here, there)]
    rows_of = [here[None, :], there[None, :]]
    held_cos, held_sin = tables(recompute_index[0].astype(F32))
    w_pair = swap(output_weight, "head", near_bit)
    slots = jnp.arange(slot_request.shape[0], dtype=jnp.int32)
    inverse = jnp.sum(jnp.where(slot_request[None, :] == slots[:, None], slots[None, :], 0), axis=1)

    first = spread(mine)
    first, new_tables, held_cos, held_sin = tie((first, new_tables, held_cos, held_sin))
    own = flat(spread(flat(pick_norm(first, slot_request, gain))))
    ka, va = prep(
        cache_lengths,
        held_states[0],
        gain,
        key_weight,
        value_weight,
        held_cos,
        held_sin,
        recompute_index,
        cache_keys[0],
        cache_values[0],
    )
    own, ka, va = tie((own, ka, va))

    far = swap(own, "head", far_bit)
    near = swap(own, "head", near_bit)
    weights = (query_weight, key_weight, value_weight)
    q_here, kn_here, vn_here = qkv([own, near], *weights, *new_tables[0])
    began = attend((0,), "cached", cache_lengths, q_here, ka, va)
    far, began = tie((far, began))
    corner = swap(far, "head", near_bit)
    q_there, kn_there, vn_there = qkv([far, corner], *weights, *new_tables[1])
    kns, vns = [kn_here, kn_there], [vn_here, vn_there]

    def turn_over(attended, kind):
        theirs = swap(attended[positions_here:], "head", near_bit)
        return project(attended[:positions_here], theirs, output_weight, w_pair, kind)

    args = (cache_lengths, q_there, ka, va, kns, vns, [there[:, None], *rows_of])
    sent = turn_over(attend((0, 1), "full", *args), BF16)
    sent, q_here = tie((sent, q_here))
    args = (cache_lengths, q_here, ka, va, kns, vns, [here[:, None], *rows_of])
    halves = [attend((0,), "new", *args, began), attend((1,), "full", *args)]
    kept = turn_over(jnp.concatenate(halves, axis=1), F32)
    got = swap(sent, "head", far_bit)
    back = spread((kept + got.astype(F32)).astype(BF16))
    returned = flat(spread(flat(pick(back, inverse))))
    hidden_out = (mine.astype(F32) + returned.astype(F32)).astype(BF16)

    away = jnp.arange(heads) ^ head

    def by_token(pieces):
        joined = jnp.concatenate(pieces, axis=0).reshape(heads, positions_here, LANES)
        return jnp.take(joined, away, axis=0).reshape(1, heads * positions_here, LANES)

    return (hidden_out[None], by_token(kns), by_token(vns))


def solution(mesh):
    return jax.shard_map(
        shards,
        mesh=mesh,
        in_specs=(
            P("req", "head", None),
            P(),
            P(None, "head"),
            P(None, "head"),
            P(None, "head"),
            P("head", None),
            P("req", None, "head"),
            P("req", None, "head"),
            P("req", None, None),
            P("req"),
            P("req", None),
            P(),
        ),
        out_specs=(P("req", "head", None), P("req", None, "head"), P("req", None, "head")),
        check_vma=False,
    )
```

```python
import functools, math
import jax
import jax.numpy as jnp
from jax import lax
from jax.experimental import pallas as pl
from jax.experimental.pallas import tpu as pltpu
from jax.sharding import PartitionSpec as P

HD = 64
LANES = 128
F32 = jnp.float32
BF16 = jnp.bfloat16
ROPE_BASE = 500000.0
MASKED = -1e30
TOP = 2.0**100
FACTOR = HD**-0.5 * math.log2(math.e)
NT = (((1,), (1,)), ((), ()))
VM = pl.BlockSpec(memory_space=pltpu.VMEM)
SM = pl.BlockSpec(memory_space=pltpu.SMEM)


def hbm(x):
    return pltpu.with_memory_space_constraint(x, pltpu.HBM)


def rms_scaled(values, gains):
    factor = lax.rsqrt(jnp.mean(values * values, axis=-1, keepdims=True) + 1e-05)
    return (values * factor * gains).astype(BF16)


def lane_of(shape):
    return lax.broadcasted_iota(jnp.int32, shape, len(shape) - 1)


def turned(x, cosine, sine):
    lane = lane_of(x.shape)
    swapped = jnp.where(
        lane % HD < HD // 2, pltpu.roll(x, LANES - HD // 2, 1), pltpu.roll(x, HD // 2, 1)
    )
    return x * cosine + swapped * sine


def head_lanes(x, which):
    return x if which == 0 else pltpu.roll(x, HD, 1)


def key_rows(k, which, bias):
    lane = lane_of(k.shape)
    tail = jnp.where(lane == HD, 1.0, jnp.where(lane == HD + 1, bias, 0.0))
    return jnp.where(lane < HD, head_lanes(k, which), tail).astype(BF16)


def value_rows(v, which):
    lane = lane_of(v.shape)
    return jnp.where(lane < HD, head_lanes(v, which), jnp.where(lane == HD, 1.0, 0.0)).astype(BF16)


def prep_kernel(length, held, gain, wk, wv, cosine, sine, index, ck, cv, ka, va, fresh):
    normed = rms_scaled(held[...].astype(F32), gain[...])
    k = jnp.dot(normed, wk[...], preferred_element_type=F32)
    fresh[:, :LANES] = turned(k, cosine[...], sine[...]).astype(BF16)
    fresh[:, LANES:] = jnp.dot(normed, wv[...], preferred_element_type=F32).astype(BF16)
    step = 512
    count = held.shape[0]

    def body(b, _):
        base = pl.multiple_of(b * step, step)
        rows = lax.broadcasted_iota(jnp.int32, (step, count), 0) + base
        hit = (rows == index[...]).astype(F32)
        placed = jnp.dot(hit.astype(BF16), fresh[...], preferred_element_type=F32)
        taken = jnp.max(hit, axis=1, keepdims=True) > 0.0
        at = pl.ds(base, step)
        kk = jnp.where(taken, placed[:, :LANES], ck[at, :].astype(F32))
        vv = jnp.where(taken, placed[:, LANES:], cv[at, :].astype(F32))
        row = lax.broadcasted_iota(jnp.int32, (step, LANES), 0) + base
        bias = jnp.where(row < length[0], 0.0, MASKED)
        for j in range(2):
            ka[j, at, :] = key_rows(kk, j, bias)
            va[j, at, :] = value_rows(vv, j)
        return 0

    lax.fori_loop(0, ck.shape[0] // step, body, 0)


def prep(length, held, gain, wk, wv, cosine, sine, index, ck, cv):
    cap = ck.shape[0]
    out = jax.ShapeDtypeStruct((2, cap, LANES), BF16)
    return pl.pallas_call(
        prep_kernel,
        out_shape=(out, out),
        in_specs=[SM] + [VM] * 9,
        out_specs=(VM, VM),
        scratch_shapes=[pltpu.VMEM((held.shape[0], 2 * LANES), BF16)],
        compiler_params=pltpu.CompilerParams(vmem_limit_bytes=40 << 20),
        cost_estimate=pl.CostEstimate(flops=3 * 10**9, bytes_accessed=8 << 20, transcendentals=0),
        name="prep",
    )(length, held, gain, wk, wv, cosine, sine, index, ck, cv)


def qkv_kernel(pieces, *refs):
    xs, refs = refs[:pieces], refs[pieces:]
    wq, wk, wv, cosine, sine, q, k, v, x, bq, bk, bv, bc, bs, done = refs
    rows = xs[0].shape[0]
    copies = [
        pltpu.make_async_copy(piece, x.at[i * rows : (i + 1) * rows, :], done.at[i])
        for i, piece in enumerate(xs)
    ]
    later = ((cosine, bc), (sine, bs), (wk, bk), (wv, bv), (wq, bq))
    for i, (w, buffer) in enumerate(later):
        copies.append(pltpu.make_async_copy(w, buffer, done.at[pieces + i]))
    for copy in copies:
        copy.start()
    for copy in copies[: pieces + 3]:
        copy.wait()
    c, s = bc[...], bs[...]
    xv = x[...]
    k[...] = turned(jnp.dot(xv, bk[...], preferred_element_type=F32), c, s).astype(BF16)
    copies[pieces + 3].wait()
    v[...] = jnp.dot(xv, bv[...], preferred_element_type=F32).astype(BF16)
    copies[pieces + 4].wait()
    for j in range(wq.shape[1] // 256):
        got = jnp.dot(xv, bq[:, j * 256 : (j + 1) * 256], preferred_element_type=F32)
        for t in range(2):
            at = slice(j * 256 + t * LANES, j * 256 + (t + 1) * LANES)
            q[:, at] = turned(got[:, t * LANES : (t + 1) * LANES], c, s).astype(BF16)


def qkv(xs, wq, wk, wv, cosine, sine):
    rows = sum(x.shape[0] for x in xs)
    depth, width = wq.shape
    out = lambda n: jax.ShapeDtypeStruct((rows, n), BF16)
    raw = pl.BlockSpec(memory_space=pltpu.HBM)
    any_place = pl.BlockSpec(memory_space=pl.ANY)
    return pl.pallas_call(
        functools.partial(qkv_kernel, len(xs)),
        out_shape=(out(width), out(LANES), out(LANES)),
        in_specs=[any_place] * len(xs) + [raw] * 5,
        out_specs=(VM,) * 3,
        scratch_shapes=[
            pltpu.VMEM((rows, depth), BF16),
            pltpu.VMEM((depth, width), BF16),
            pltpu.VMEM((depth, LANES), BF16),
            pltpu.VMEM((depth, LANES), BF16),
            pltpu.VMEM((rows, LANES), F32),
            pltpu.VMEM((rows, LANES), F32),
            pltpu.SemaphoreType.DMA((len(xs) + 5,)),
        ],
        compiler_params=pltpu.CompilerParams(vmem_limit_bytes=16 << 20),
        cost_estimate=pl.CostEstimate(
            flops=2 * rows * depth * (width + 2 * LANES), bytes_accessed=5 << 20, transcendentals=0
        ),
        name="qkv",
    )(*xs, hbm(wq), hbm(wk), hbm(wv), hbm(cosine), hbm(sine))


KEYS = 1024
ROWS = 1024
PARTS = 2


def att_kernel(chunks, which, js, mode, scal, q, ka, va, *refs):
    refs = list(refs)
    take_refs = lambda count: [refs.pop(0) for _ in range(count)]
    if mode != "cached":
        kn, vn = take_refs(chunks), take_refs(chunks)
    if mode == "new":
        qa_in, acc_in = take_refs(2)
    if mode == "cached":
        qa_out, acc_out = take_refs(2)
    else:
        (o,) = take_refs(1)
    if mode != "cached":
        qa_s, acc_s, na, nv, low = take_refs(5)
    if mode == "new":
        kbuf, vbuf = take_refs(2)
    tokens = q.shape[0]
    length = scal[0]
    per = q.shape[1] // HD // 2
    rows = per * tokens
    blocks = lax.div(length + (KEYS - 1), KEYS)
    lane = lane_of((tokens, LANES))
    spans = [slice(g * tokens, (g + 1) * tokens) for g in range(per)]

    if mode != "cached":
        owned = tokens // 2

        def position(block, axis):
            i = lax.broadcasted_iota(jnp.int32, (tokens, tokens), axis)
            return i + jnp.where(i < owned, scal[1 + 2 * block], scal[2 + 2 * block] - owned)

        allowed = [position(block, 1) <= position(which, 0) for block in range(chunks)]

    for n, j in enumerate(js):
        if mode == "cached":
            qa, acc = qa_out.at[n], acc_out.at[n]
        else:
            qa, acc = qa_s, acc_s

        def put_queries(g, offset):
            pair = (j * per + g) // 2
            x = q[:, pair * LANES : (pair + 1) * LANES].astype(F32)
            tail = jnp.where(lane == HD, offset, jnp.where(lane == HD + 1, 1.0, 0.0))
            qa[spans[g], :] = jnp.where(lane < HD, head_lanes(x, g % 2), tail).astype(BF16)

        def weights(keys, at):
            s = lax.dot_general(qa[at, :], keys, NT, preferred_element_type=F32)
            return jnp.exp2(s * FACTOR)

        if mode == "new":
            qa[...] = qa_in[n]
            acc[...] = acc_in[n]
        else:
            for g in range(per):
                put_queries(g, 0.0)
                first = lax.dot_general(
                    qa[spans[g], :], ka[j, :256, :], NT, preferred_element_type=F32
                )
                put_queries(g, -jnp.max(first, axis=1, keepdims=True))
            acc[...] = jnp.zeros(acc.shape, F32)

        if mode != "cached":
            for part in range(chunks):
                na[part] = key_rows(kn[part][...].astype(F32), j, 0.0)
                nv[part] = value_rows(vn[part][...].astype(F32), j)
            for g in range(per):
                total = acc[spans[g], :]
                for part in range(chunks):
                    p = jnp.where(allowed[part], weights(na[part], spans[g]), 0.0)
                    total += jnp.dot(p.astype(BF16), nv[part], preferred_element_type=F32)
                acc[spans[g], :] = total

        if mode != "new":

            def body(b, _):
                at = pl.ds(pl.multiple_of(b * KEYS, KEYS), KEYS)
                keys, values = ka[j, at, :], va[j, at, :]
                for r in range(rows // ROWS):
                    q_at = slice(r * ROWS, (r + 1) * ROWS)
                    p = weights(keys, q_at).astype(BF16)
                    acc[q_at, :] += jnp.dot(p, values, preferred_element_type=F32)
                return 0

            lax.fori_loop(0, blocks, body, 0)

        if mode == "cached":
            continue

        safe = jnp.min((acc[:, HD : HD + 1] < TOP).astype(F32)) > 0.5

        @pl.when(jnp.logical_not(safe))
        def _():
            if mode == "new":
                pltpu.sync_copy(ka.at[j], kbuf)
                pltpu.sync_copy(va.at[j], vbuf)
                old_k, old_v = kbuf, vbuf
            else:
                old_k, old_v = ka.at[j], va.at[j]
            for g in range(per):
                put_queries(g, 0.0)
            acc[...] = jnp.zeros(acc.shape, F32)
            low[...] = jnp.full(low.shape, MASKED, F32)

            def take(keys, values, permitted, at):
                s = lax.dot_general(qa[at, :], keys, NT, preferred_element_type=F32)
                if permitted is not None:
                    s = jnp.where(permitted, s, MASKED)
                past = low[at, :]
                top = jnp.maximum(past, jnp.max(s, axis=1, keepdims=True))
                p = jnp.exp2((s - top[:, :1]) * FACTOR)
                shrink = jnp.exp2((past - top) * FACTOR)
                low[at, :] = top
                acc[at, :] = acc[at, :] * shrink + jnp.dot(
                    p.astype(BF16), values, preferred_element_type=F32
                )

            def redo(b, _):
                at = pl.ds(pl.multiple_of(b * 512, 512), 512)
                for g in range(per):
                    take(old_k[at, :], old_v[at, :], None, spans[g])
                return 0

            lax.fori_loop(0, lax.div(length + 511, 512), redo, 0)
            for g in range(per):
                for part in range(chunks):
                    take(na[part], nv[part], allowed[part], spans[g])

        for g in range(0, per, 2):
            pair = []
            for t in range(2):
                got = acc[spans[g + t], :]
                pair.append(got / got[:, HD : HD + 1])
            at = slice((n * per + g) * HD, (n * per + g + 2) * HD)
            o[:, at] = jnp.where(lane < HD, pair[0], pltpu.roll(pair[1], HD, 1)).astype(BF16)


def attend(which, js, mode, scal, q, ka, va, kns=(), vns=(), began=()):
    tokens, chunks = q.shape[0], PARTS
    rows = q.shape[1] // HD // 2 * tokens
    keys = {"cached": ka.shape[1], "new": tokens * chunks, "full": ka.shape[1] + tokens * chunks}[mode]
    scratch = []
    if mode != "cached":
        scratch = [
            pltpu.VMEM((rows, LANES), BF16),
            pltpu.VMEM((rows, LANES), F32),
            pltpu.VMEM((chunks, tokens, LANES), BF16),
            pltpu.VMEM((chunks, tokens, LANES), BF16),
            pltpu.VMEM((rows, LANES), F32),
        ]
    cached = VM
    if mode == "new":
        scratch += [pltpu.VMEM(ka.shape[1:], BF16)] * 2
        cached = pl.BlockSpec(memory_space=pl.ANY)
    if mode == "cached":
        shape = (len(js), rows, LANES)
        out = (jax.ShapeDtypeStruct(shape, BF16), jax.ShapeDtypeStruct(shape, F32))
        specs = (VM, VM)
    else:
        out = jax.ShapeDtypeStruct((tokens, q.shape[1] // 2 * len(js)), BF16)
        specs = VM
    return pl.pallas_call(
        functools.partial(att_kernel, chunks, which, js, mode),
        out_shape=out,
        in_specs=[SM, VM, cached, cached] + [VM] * (len(kns) + len(vns) + len(began)),
        out_specs=specs,
        scratch_shapes=scratch,
        compiler_params=pltpu.CompilerParams(vmem_limit_bytes=32 << 20),
        cost_estimate=pl.CostEstimate(
            flops=4 * rows * len(js) * keys * 256,
            bytes_accessed=4 << 20,
            transcendentals=rows * len(js) * keys,
        ),
        name="attend_" + mode,
    )(scal, q, ka, va, *kns, *vns, *began)


def tables(positions):
    ladder = jnp.arange(HD // 2).astype(F32)
    frequency = jnp.exp(ladder * (-2.0 * math.log(ROPE_BASE) / HD))
    angles = positions[:, None] * frequency
    cosine, sine = jnp.cos(angles), jnp.sin(angles)
    return (
        jnp.concatenate([cosine] * 4, axis=-1),
        jnp.concatenate([-sine, sine, -sine, sine], axis=-1),
    )


def pick_kernel(order, x, out, done):
    count = out.shape[0]
    copies = [pltpu.make_async_copy(x.at[order[s]], out.at[s], done.at[s]) for s in range(count)]
    for copy in copies:
        copy.start()
    for copy in copies:
        copy.wait()


def pick(x, order):
    return pl.pallas_call(
        pick_kernel,
        out_shape=jax.ShapeDtypeStruct(x.shape, x.dtype),
        in_specs=[SM, pl.BlockSpec(memory_space=pl.ANY)],
        out_specs=pl.BlockSpec(memory_space=pl.ANY),
        scratch_shapes=[pltpu.SemaphoreType.DMA((x.shape[0],))],
        compiler_params=pltpu.CompilerParams(vmem_limit_bytes=1 << 20),
        name="pick",
    )(order, x)


def pick_norm_kernel(order, x, gain, out):
    for s in range(out.shape[0]):
        out[s] = rms_scaled(x[order[s]].astype(F32), gain[...])


def pick_norm(x, order, gain):
    return pl.pallas_call(
        pick_norm_kernel,
        out_shape=jax.ShapeDtypeStruct(x.shape, x.dtype),
        in_specs=[SM, VM, VM],
        out_specs=VM,
        compiler_params=pltpu.CompilerParams(vmem_limit_bytes=8 << 20),
        name="pick_norm",
    )(order, x, gain)


def project_kernel(mine, theirs, w, w_pair, out):
    terms = [
        jnp.dot(x[...], y[...], preferred_element_type=F32).astype(BF16).astype(F32)
        for x, y in ((mine, w), (theirs, w_pair))
    ]
    out[...] = (terms[0] + terms[1]).astype(out.dtype)


def project(mine, theirs, w, w_pair, kind):
    rows, depth = mine.shape
    width = w.shape[1]
    step = 1024
    return pl.pallas_call(
        project_kernel,
        out_shape=jax.ShapeDtypeStruct((rows, width), kind),
        grid=(width // step,),
        in_specs=[pl.BlockSpec((rows, depth), lambda n: (0, 0))] * 2
        + [pl.BlockSpec((depth, step), lambda n: (0, n))] * 2,
        out_specs=pl.BlockSpec((rows, step), lambda n: (0, n)),
        compiler_params=pltpu.CompilerParams(vmem_limit_bytes=16 << 20),
        cost_estimate=pl.CostEstimate(
            flops=4 * rows * depth * width, bytes_accessed=6 << 20, transcendentals=0
        ),
        name="project",
    )(mine, theirs, w, w_pair)


def swap(x, axis, bits):
    size = lax.axis_size(axis)
    return lax.ppermute(x, axis, [(i, i ^ bits) for i in range(size)])


def spread(x):
    groups = lax.axis_size("req")
    rows, features = x.shape
    pieces = x.reshape(groups, rows // groups, features)
    return lax.all_to_all(pieces, "req", split_axis=0, concat_axis=0, tiled=True)


def shards(
    hidden_in,
    norm_gain,
    query_weight,
    key_weight,
    value_weight,
    output_weight,
    cache_keys,
    cache_values,
    held_states,
    cache_lengths,
    recompute_index,
    slot_request,
):
    requests_here, positions_here, features = hidden_in.shape
    assert requests_here == 1
    heads = lax.axis_size("head")
    head = lax.axis_index("head")
    mine = hidden_in[0]
    gain = norm_gain[None, :]
    length = cache_lengths[0]
    tie = lax.optimization_barrier
    flat = lambda x: x.reshape(positions_here, features)
    far_bit, near_bit = heads // 2, 1
    inner = jnp.arange(positions_here)
    place = lambda bits: jnp.concatenate(
        [(head ^ bit) * positions_here + inner for bit in bits]
    ).astype(jnp.int32)
    here, there = place((0, near_bit)), place((far_bit, far_bit + near_bit))
    new_tables = [tables(length.astype(F32) + x.astype(F32)) for x in (here, there)]
    bits = (0, near_bit, far_bit, far_bit + near_bit)
    scal = jnp.stack([length] + [((head ^ bit) * positions_here).astype(jnp.int32) for bit in bits])
    held_cos, held_sin = tables(recompute_index[0].astype(F32))
    w_pair = swap(output_weight, "head", near_bit)
    slots = jnp.arange(slot_request.shape[0], dtype=jnp.int32)
    inverse = jnp.sum(jnp.where(slot_request[None, :] == slots[:, None], slots[None, :], 0), axis=1)

    first = spread(mine)
    first, new_tables, held_cos, held_sin = tie((first, new_tables, held_cos, held_sin))
    own = flat(spread(flat(pick_norm(first, slot_request, gain))))
    ka, va = prep(
        cache_lengths,
        held_states[0],
        gain,
        key_weight,
        value_weight,
        held_cos,
        held_sin,
        recompute_index,
        cache_keys[0],
        cache_values[0],
    )
    own, ka, va = tie((own, ka, va))

    far = swap(own, "head", far_bit)
    near = swap(own, "head", near_bit)
    weights = (query_weight, key_weight, value_weight)
    q_here, kn_here, vn_here = qkv([own, near], *weights, *new_tables[0])
    began = attend(0, (0,), "cached", scal, q_here, ka, va)
    far, began = tie((far, began))
    corner = swap(far, "head", near_bit)
    q_there, kn_there, vn_there = qkv([far, corner], *weights, *new_tables[1])
    kns, vns = [kn_here, kn_there], [vn_here, vn_there]

    def turn_over(attended, kind):
        theirs = swap(attended[positions_here:], "head", near_bit)
        return project(attended[:positions_here], theirs, output_weight, w_pair, kind)

    args = (scal, q_there, ka, va, kns, vns)
    sent = turn_over(attend(1, (0, 1), "full", *args), BF16)
    sent, q_here = tie((sent, q_here))
    args = (scal, q_here, ka, va, kns, vns)
    halves = [attend(0, (0,), "new", *args, began), attend(0, (1,), "full", *args)]
    kept = turn_over(jnp.concatenate(halves, axis=1), F32)
    got = swap(sent, "head", far_bit)
    back = spread((kept + got.astype(F32)).astype(BF16))
    returned = flat(spread(flat(pick(back, inverse))))
    hidden_out = (mine.astype(F32) + returned.astype(F32)).astype(BF16)

    away = jnp.arange(heads) ^ head

    def by_token(pieces):
        joined = jnp.concatenate(pieces, axis=0).reshape(heads, positions_here, LANES)
        return jnp.take(joined, away, axis=0).reshape(1, heads * positions_here, LANES)

    return (hidden_out[None], by_token(kns), by_token(vns))


def solution(mesh):
    return jax.shard_map(
        shards,
        mesh=mesh,
        in_specs=(
            P("req", "head", None),
            P(),
            P(None, "head"),
            P(None, "head"),
            P(None, "head"),
            P("head", None),
            P("req", None, "head"),
            P("req", None, "head"),
            P("req", None, None),
            P("req"),
            P("req", None),
            P(),
        ),
        out_specs=(P("req", "head", None), P("req", None, "head"), P("req", None, "head")),
        check_vma=False,
    )
```

```python
import functools, math
import jax
import jax.numpy as jnp
from jax import lax
from jax.experimental import pallas as pl
from jax.experimental.pallas import tpu as pltpu
from jax.sharding import PartitionSpec as P

HD = 64
LANES = 128
F32 = jnp.float32
BF16 = jnp.bfloat16
ROPE_BASE = 500000.0
MASKED = -1e30
TOP = 2.0**100
FACTOR = HD**-0.5 * math.log2(math.e)
NT = (((1,), (1,)), ((), ()))
VM = pl.BlockSpec(memory_space=pltpu.VMEM)
SM = pl.BlockSpec(memory_space=pltpu.SMEM)


def hbm(x):
    return pltpu.with_memory_space_constraint(x, pltpu.HBM)


def rms_scaled(values, gains):
    factor = lax.rsqrt(jnp.mean(values * values, axis=-1, keepdims=True) + 1e-05)
    return (values * factor * gains).astype(BF16)


def lane_of(shape):
    return lax.broadcasted_iota(jnp.int32, shape, len(shape) - 1)


def turned(x, cosine, sine):
    lane = lane_of(x.shape)
    swapped = jnp.where(
        lane % HD < HD // 2, pltpu.roll(x, LANES - HD // 2, 1), pltpu.roll(x, HD // 2, 1)
    )
    return x * cosine + swapped * sine


def head_lanes(x, which):
    return x if which == 0 else pltpu.roll(x, HD, 1)


def key_rows(k, which, bias):
    lane = lane_of(k.shape)
    tail = jnp.where(lane == HD, 1.0, jnp.where(lane == HD + 1, bias, 0.0))
    return jnp.where(lane < HD, head_lanes(k, which), tail).astype(BF16)


def value_rows(v, which):
    lane = lane_of(v.shape)
    return jnp.where(lane < HD, head_lanes(v, which), jnp.where(lane == HD, 1.0, 0.0)).astype(BF16)


def prep_kernel(length, held, gain, wk, wv, cosine, sine, index, ck, cv, ka, va, fresh):
    normed = rms_scaled(held[...].astype(F32), gain[...])
    k = jnp.dot(normed, wk[...], preferred_element_type=F32)
    fresh[:, :LANES] = turned(k, cosine[...], sine[...]).astype(BF16)
    fresh[:, LANES:] = jnp.dot(normed, wv[...], preferred_element_type=F32).astype(BF16)
    step = 512
    count = held.shape[0]

    def body(b, _):
        base = pl.multiple_of(b * step, step)
        rows = lax.broadcasted_iota(jnp.int32, (step, count), 0) + base
        hit = (rows == index[...]).astype(F32)
        placed = jnp.dot(hit.astype(BF16), fresh[...], preferred_element_type=F32)
        taken = jnp.max(hit, axis=1, keepdims=True) > 0.0
        at = pl.ds(base, step)
        kk = jnp.where(taken, placed[:, :LANES], ck[at, :].astype(F32))
        vv = jnp.where(taken, placed[:, LANES:], cv[at, :].astype(F32))
        row = lax.broadcasted_iota(jnp.int32, (step, LANES), 0) + base
        bias = jnp.where(row < length[0], 0.0, MASKED)
        for j in range(2):
            ka[j, at, :] = key_rows(kk, j, bias)
            va[j, at, :] = value_rows(vv, j)
        return 0

    lax.fori_loop(0, ck.shape[0] // step, body, 0)


def prep(length, held, gain, wk, wv, cosine, sine, index, ck, cv):
    cap = ck.shape[0]
    out = jax.ShapeDtypeStruct((2, cap, LANES), BF16)
    return pl.pallas_call(
        prep_kernel,
        out_shape=(out, out),
        in_specs=[SM] + [VM] * 9,
        out_specs=(VM, VM),
        scratch_shapes=[pltpu.VMEM((held.shape[0], 2 * LANES), BF16)],
        compiler_params=pltpu.CompilerParams(vmem_limit_bytes=40 << 20),
        cost_estimate=pl.CostEstimate(flops=3 * 10**9, bytes_accessed=8 << 20, transcendentals=0),
        name="prep",
    )(length, held, gain, wk, wv, cosine, sine, index, ck, cv)


def qkv_kernel(pieces, *refs):
    xs, refs = refs[:pieces], refs[pieces:]
    wq, wk, wv, cosine, sine, q, k, v, x, bq, bk, bv, bc, bs, done = refs
    rows = xs[0].shape[0]
    copies = [
        pltpu.make_async_copy(piece, x.at[i * rows : (i + 1) * rows, :], done.at[i])
        for i, piece in enumerate(xs)
    ]
    later = ((cosine, bc), (sine, bs), (wk, bk), (wv, bv), (wq, bq))
    for i, (w, buffer) in enumerate(later):
        copies.append(pltpu.make_async_copy(w, buffer, done.at[pieces + i]))
    for copy in copies:
        copy.start()
    for copy in copies[: pieces + 3]:
        copy.wait()
    c, s = bc[...], bs[...]
    xv = x[...]
    k[...] = turned(jnp.dot(xv, bk[...], preferred_element_type=F32), c, s).astype(BF16)
    copies[pieces + 3].wait()
    v[...] = jnp.dot(xv, bv[...], preferred_element_type=F32).astype(BF16)
    copies[pieces + 4].wait()
    for j in range(wq.shape[1] // 256):
        got = jnp.dot(xv, bq[:, j * 256 : (j + 1) * 256], preferred_element_type=F32)
        for t in range(2):
            at = slice(j * 256 + t * LANES, j * 256 + (t + 1) * LANES)
            q[:, at] = turned(got[:, t * LANES : (t + 1) * LANES], c, s).astype(BF16)


def qkv(xs, wq, wk, wv, cosine, sine):
    rows = sum(x.shape[0] for x in xs)
    depth, width = wq.shape
    out = lambda n: jax.ShapeDtypeStruct((rows, n), BF16)
    raw = pl.BlockSpec(memory_space=pltpu.HBM)
    any_place = pl.BlockSpec(memory_space=pl.ANY)
    return pl.pallas_call(
        functools.partial(qkv_kernel, len(xs)),
        out_shape=(out(width), out(LANES), out(LANES)),
        in_specs=[any_place] * len(xs) + [raw] * 5,
        out_specs=(VM,) * 3,
        scratch_shapes=[
            pltpu.VMEM((rows, depth), BF16),
            pltpu.VMEM((depth, width), BF16),
            pltpu.VMEM((depth, LANES), BF16),
            pltpu.VMEM((depth, LANES), BF16),
            pltpu.VMEM((rows, LANES), F32),
            pltpu.VMEM((rows, LANES), F32),
            pltpu.SemaphoreType.DMA((len(xs) + 5,)),
        ],
        compiler_params=pltpu.CompilerParams(vmem_limit_bytes=16 << 20),
        cost_estimate=pl.CostEstimate(
            flops=2 * rows * depth * (width + 2 * LANES), bytes_accessed=5 << 20, transcendentals=0
        ),
        name="qkv",
    )(*xs, hbm(wq), hbm(wk), hbm(wv), hbm(cosine), hbm(sine))


KEYS = 2048
ROWS = 1024
PARTS = 2


def att_kernel(chunks, which, js, mode, scal, q, ka, va, *refs):
    refs = list(refs)
    take_refs = lambda count: [refs.pop(0) for _ in range(count)]
    if mode != "cached":
        kn, vn = take_refs(chunks), take_refs(chunks)
    if mode == "new":
        qa_in, acc_in = take_refs(2)
    if mode == "cached":
        qa_out, acc_out = take_refs(2)
    else:
        (o,) = take_refs(1)
    if mode != "cached":
        qa_s, acc_s, na, nv, low = take_refs(5)
    if mode == "new":
        kbuf, vbuf = take_refs(2)
    tokens = q.shape[0]
    length = scal[0]
    per = q.shape[1] // HD // 2
    rows = per * tokens
    blocks = lax.div(length + (KEYS - 1), KEYS)
    lane = lane_of((tokens, LANES))
    spans = [slice(g * tokens, (g + 1) * tokens) for g in range(per)]

    if mode != "cached":
        owned = tokens // 2

        def position(block, axis):
            i = lax.broadcasted_iota(jnp.int32, (tokens, tokens), axis)
            return i + jnp.where(i < owned, scal[1 + 2 * block], scal[2 + 2 * block] - owned)

        allowed = [position(block, 1) <= position(which, 0) for block in range(chunks)]

    for n, j in enumerate(js):
        if mode == "cached":
            qa, acc = qa_out.at[n], acc_out.at[n]
        else:
            qa, acc = qa_s, acc_s

        def put_queries(g, offset):
            pair = (j * per + g) // 2
            x = q[:, pair * LANES : (pair + 1) * LANES].astype(F32)
            tail = jnp.where(lane == HD, offset, jnp.where(lane == HD + 1, 1.0, 0.0))
            qa[spans[g], :] = jnp.where(lane < HD, head_lanes(x, g % 2), tail).astype(BF16)

        def weights(keys, at):
            s = lax.dot_general(qa[at, :], keys, NT, preferred_element_type=F32)
            return jnp.exp2(s * FACTOR)

        if mode == "new":
            qa[...] = qa_in[n]
            acc[...] = acc_in[n]
        else:
            for g in range(per):
                put_queries(g, 0.0)
                first = lax.dot_general(
                    qa[spans[g], :], ka[j, :256, :], NT, preferred_element_type=F32
                )
                put_queries(g, -jnp.max(first, axis=1, keepdims=True))
            acc[...] = jnp.zeros(acc.shape, F32)

        if mode != "cached":
            for part in range(chunks):
                na[part] = key_rows(kn[part][...].astype(F32), j, 0.0)
                nv[part] = value_rows(vn[part][...].astype(F32), j)
            for g in range(per):
                total = acc[spans[g], :]
                for part in range(chunks):
                    p = jnp.where(allowed[part], weights(na[part], spans[g]), 0.0)
                    total += jnp.dot(p.astype(BF16), nv[part], preferred_element_type=F32)
                acc[spans[g], :] = total

        if mode != "new":

            def body(b, _):
                at = pl.ds(pl.multiple_of(b * KEYS, KEYS), KEYS)
                keys, values = ka[j, at, :], va[j, at, :]
                for r in range(rows // ROWS):
                    q_at = slice(r * ROWS, (r + 1) * ROWS)
                    p = weights(keys, q_at).astype(BF16)
                    acc[q_at, :] += jnp.dot(p, values, preferred_element_type=F32)
                return 0

            lax.fori_loop(0, blocks, body, 0)

        if mode == "cached":
            continue

        safe = jnp.min((acc[:, HD : HD + 1] < TOP).astype(F32)) > 0.5

        @pl.when(jnp.logical_not(safe))
        def _():
            if mode == "new":
                pltpu.sync_copy(ka.at[j], kbuf)
                pltpu.sync_copy(va.at[j], vbuf)
                old_k, old_v = kbuf, vbuf
            else:
                old_k, old_v = ka.at[j], va.at[j]
            for g in range(per):
                put_queries(g, 0.0)
            acc[...] = jnp.zeros(acc.shape, F32)
            low[...] = jnp.full(low.shape, MASKED, F32)

            def take(keys, values, permitted, at):
                s = lax.dot_general(qa[at, :], keys, NT, preferred_element_type=F32)
                if permitted is not None:
                    s = jnp.where(permitted, s, MASKED)
                past = low[at, :]
                top = jnp.maximum(past, jnp.max(s, axis=1, keepdims=True))
                p = jnp.exp2((s - top[:, :1]) * FACTOR)
                shrink = jnp.exp2((past - top) * FACTOR)
                low[at, :] = top
                acc[at, :] = acc[at, :] * shrink + jnp.dot(
                    p.astype(BF16), values, preferred_element_type=F32
                )

            def redo(b, _):
                at = pl.ds(pl.multiple_of(b * 512, 512), 512)
                for g in range(per):
                    take(old_k[at, :], old_v[at, :], None, spans[g])
                return 0

            lax.fori_loop(0, lax.div(length + 511, 512), redo, 0)
            for g in range(per):
                for part in range(chunks):
                    take(na[part], nv[part], allowed[part], spans[g])

        for g in range(0, per, 2):
            pair = []
            for t in range(2):
                got = acc[spans[g + t], :]
                pair.append(got / got[:, HD : HD + 1])
            at = slice((n * per + g) * HD, (n * per + g + 2) * HD)
            o[:, at] = jnp.where(lane < HD, pair[0], pltpu.roll(pair[1], HD, 1)).astype(BF16)


def attend(which, js, mode, scal, q, ka, va, kns=(), vns=(), began=()):
    tokens, chunks = q.shape[0], PARTS
    rows = q.shape[1] // HD // 2 * tokens
    keys = {"cached": ka.shape[1], "new": tokens * chunks, "full": ka.shape[1] + tokens * chunks}[mode]
    scratch = []
    if mode != "cached":
        scratch = [
            pltpu.VMEM((rows, LANES), BF16),
            pltpu.VMEM((rows, LANES), F32),
            pltpu.VMEM((chunks, tokens, LANES), BF16),
            pltpu.VMEM((chunks, tokens, LANES), BF16),
            pltpu.VMEM((rows, LANES), F32),
        ]
    cached = VM
    if mode == "new":
        scratch += [pltpu.VMEM(ka.shape[1:], BF16)] * 2
        cached = pl.BlockSpec(memory_space=pl.ANY)
    if mode == "cached":
        shape = (len(js), rows, LANES)
        out = (jax.ShapeDtypeStruct(shape, BF16), jax.ShapeDtypeStruct(shape, F32))
        specs = (VM, VM)
    else:
        out = jax.ShapeDtypeStruct((tokens, q.shape[1] // 2 * len(js)), BF16)
        specs = VM
    return pl.pallas_call(
        functools.partial(att_kernel, chunks, which, js, mode),
        out_shape=out,
        in_specs=[SM, VM, cached, cached] + [VM] * (len(kns) + len(vns) + len(began)),
        out_specs=specs,
        scratch_shapes=scratch,
        compiler_params=pltpu.CompilerParams(vmem_limit_bytes=32 << 20),
        cost_estimate=pl.CostEstimate(
            flops=4 * rows * len(js) * keys * 256,
            bytes_accessed=4 << 20,
            transcendentals=rows * len(js) * keys,
        ),
        name="attend_" + mode,
    )(scal, q, ka, va, *kns, *vns, *began)


def tables(positions):
    ladder = jnp.arange(HD // 2).astype(F32)
    frequency = jnp.exp(ladder * (-2.0 * math.log(ROPE_BASE) / HD))
    angles = positions[:, None] * frequency
    cosine, sine = jnp.cos(angles), jnp.sin(angles)
    return (
        jnp.concatenate([cosine] * 4, axis=-1),
        jnp.concatenate([-sine, sine, -sine, sine], axis=-1),
    )


def pick_kernel(order, x, out, done):
    count = out.shape[0]
    copies = [pltpu.make_async_copy(x.at[order[s]], out.at[s], done.at[s]) for s in range(count)]
    for copy in copies:
        copy.start()
    for copy in copies:
        copy.wait()


def pick(x, order):
    return pl.pallas_call(
        pick_kernel,
        out_shape=jax.ShapeDtypeStruct(x.shape, x.dtype),
        in_specs=[SM, pl.BlockSpec(memory_space=pl.ANY)],
        out_specs=pl.BlockSpec(memory_space=pl.ANY),
        scratch_shapes=[pltpu.SemaphoreType.DMA((x.shape[0],))],
        compiler_params=pltpu.CompilerParams(vmem_limit_bytes=1 << 20),
        name="pick",
    )(order, x)


def pick_norm_kernel(order, x, gain, out):
    for s in range(out.shape[0]):
        out[s] = rms_scaled(x[order[s]].astype(F32), gain[...])


def pick_norm(x, order, gain):
    return pl.pallas_call(
        pick_norm_kernel,
        out_shape=jax.ShapeDtypeStruct(x.shape, x.dtype),
        in_specs=[SM, VM, VM],
        out_specs=VM,
        compiler_params=pltpu.CompilerParams(vmem_limit_bytes=8 << 20),
        name="pick_norm",
    )(order, x, gain)


def project_kernel(mine, theirs, w, w_pair, out):
    terms = [
        jnp.dot(x[...], y[...], preferred_element_type=F32).astype(BF16).astype(F32)
        for x, y in ((mine, w), (theirs, w_pair))
    ]
    out[...] = (terms[0] + terms[1]).astype(out.dtype)


def project(mine, theirs, w, w_pair, kind):
    rows, depth = mine.shape
    width = w.shape[1]
    step = 1024
    return pl.pallas_call(
        project_kernel,
        out_shape=jax.ShapeDtypeStruct((rows, width), kind),
        grid=(width // step,),
        in_specs=[pl.BlockSpec((rows, depth), lambda n: (0, 0))] * 2
        + [pl.BlockSpec((depth, step), lambda n: (0, n))] * 2,
        out_specs=pl.BlockSpec((rows, step), lambda n: (0, n)),
        compiler_params=pltpu.CompilerParams(vmem_limit_bytes=16 << 20),
        cost_estimate=pl.CostEstimate(
            flops=4 * rows * depth * width, bytes_accessed=6 << 20, transcendentals=0
        ),
        name="project",
    )(mine, theirs, w, w_pair)


def swap(x, axis, bits):
    size = lax.axis_size(axis)
    return lax.ppermute(x, axis, [(i, i ^ bits) for i in range(size)])


def spread(x):
    groups = lax.axis_size("req")
    rows, features = x.shape
    pieces = x.reshape(groups, rows // groups, features)
    return lax.all_to_all(pieces, "req", split_axis=0, concat_axis=0, tiled=True)


def shards(
    hidden_in,
    norm_gain,
    query_weight,
    key_weight,
    value_weight,
    output_weight,
    cache_keys,
    cache_values,
    held_states,
    cache_lengths,
    recompute_index,
    slot_request,
):
    requests_here, positions_here, features = hidden_in.shape
    assert requests_here == 1
    heads = lax.axis_size("head")
    head = lax.axis_index("head")
    mine = hidden_in[0]
    gain = norm_gain[None, :]
    length = cache_lengths[0]
    tie = lax.optimization_barrier
    flat = lambda x: x.reshape(positions_here, features)
    far_bit, near_bit = heads // 2, 1
    inner = jnp.arange(positions_here)
    place = lambda bits: jnp.concatenate(
        [(head ^ bit) * positions_here + inner for bit in bits]
    ).astype(jnp.int32)
    here, there = place((0, near_bit)), place((far_bit, far_bit + near_bit))
    new_tables = [tables(length.astype(F32) + x.astype(F32)) for x in (here, there)]
    bits = (0, near_bit, far_bit, far_bit + near_bit)
    scal = jnp.stack([length] + [((head ^ bit) * positions_here).astype(jnp.int32) for bit in bits])
    held_cos, held_sin = tables(recompute_index[0].astype(F32))
    w_pair = swap(output_weight, "head", near_bit)
    slots = jnp.arange(slot_request.shape[0], dtype=jnp.int32)
    inverse = jnp.sum(jnp.where(slot_request[None, :] == slots[:, None], slots[None, :], 0), axis=1)

    first = spread(mine)
    first, new_tables, held_cos, held_sin = tie((first, new_tables, held_cos, held_sin))
    own = flat(spread(flat(pick_norm(first, slot_request, gain))))
    ka, va = prep(
        cache_lengths,
        held_states[0],
        gain,
        key_weight,
        value_weight,
        held_cos,
        held_sin,
        recompute_index,
        cache_keys[0],
        cache_values[0],
    )
    own, ka, va = tie((own, ka, va))

    far = swap(own, "head", far_bit)
    near = swap(own, "head", near_bit)
    weights = (query_weight, key_weight, value_weight)
    q_here, kn_here, vn_here = qkv([own, near], *weights, *new_tables[0])
    began = attend(0, (0,), "cached", scal, q_here, ka, va)
    far, began = tie((far, began))
    corner = swap(far, "head", near_bit)
    q_there, kn_there, vn_there = qkv([far, corner], *weights, *new_tables[1])
    kns, vns = [kn_here, kn_there], [vn_here, vn_there]

    def turn_over(attended, kind):
        theirs = swap(attended[positions_here:], "head", near_bit)
        return project(attended[:positions_here], theirs, output_weight, w_pair, kind)

    args = (scal, q_there, ka, va, kns, vns)
    sent = turn_over(attend(1, (0, 1), "full", *args), BF16)
    sent, q_here = tie((sent, q_here))
    args = (scal, q_here, ka, va, kns, vns)
    halves = [attend(0, (0,), "new", *args, began), attend(0, (1,), "full", *args)]
    kept = turn_over(jnp.concatenate(halves, axis=1), F32)
    got = swap(sent, "head", far_bit)
    back = spread((kept + got.astype(F32)).astype(BF16))
    returned = flat(spread(flat(pick(back, inverse))))
    hidden_out = (mine.astype(F32) + returned.astype(F32)).astype(BF16)

    away = jnp.arange(heads) ^ head

    def by_token(pieces):
        joined = jnp.concatenate(pieces, axis=0).reshape(heads, positions_here, LANES)
        return jnp.take(joined, away, axis=0).reshape(1, heads * positions_here, LANES)

    return (hidden_out[None], by_token(kns), by_token(vns))


def solution(mesh):
    return jax.shard_map(
        shards,
        mesh=mesh,
        in_specs=(
            P("req", "head", None),
            P(),
            P(None, "head"),
            P(None, "head"),
            P(None, "head"),
            P("head", None),
            P("req", None, "head"),
            P("req", None, "head"),
            P("req", None, None),
            P("req"),
            P("req", None),
            P(),
        ),
        out_specs=(P("req", "head", None), P("req", None, "head"), P("req", None, "head")),
        check_vma=False,
    )
```
